32 devices in a mesh: section: 8 (over y, x, core), dp: 4 (over z).
Axes of the slice: x: 2, y: 2, z: 4, core: 2. Of those that a mesh axis runs over, the one named last changes fastest.
Arguments:
- activations: bfloat16 [2048, 8192], P('dp'), may hold values from -6 to 6
- cotangent: bfloat16 [2048, 8192], P('dp'), may hold values from -6 to 6
- gate_pre: bfloat16 [2048, 4096], P('dp', 'section'), may hold values from -6 to 6
- weights: bfloat16 [2, 8192, 4096], P(None, 'dp', 'section'), may hold values from -0.0625 to 0.0625
- holder_map: int32 [64, 8, 2], P('dp', 'section'), may hold values from 0 to 7, as said below
- master: float32 [8, 4, 48, 128, 512], P('section', 'dp'), may hold values from -0.0625 to 0.0625
- moment_one: float32 [8, 4, 48, 128, 512], P('section', 'dp'), may hold values from -80 to 80
- moment_two: float32 [8, 4, 48, 128, 512], P('section', 'dp'), may hold values from 102.4 to 4096
- adam_step: int32 [1], replicated, may hold values from 1 to 11
Outputs:
- passed_back: bfloat16 [2048, 8192], P('dp', 'section')
- new_weights: bfloat16 [2, 8192, 4096], P(None, 'dp', 'section')
The draws below stay inside these ranges and needn't reach their ends.
Inputs may be any that keep to these rules, and one draw needn't show every extreme that they name: `holder_map`: every block of one device (32 of them) goes to holders of that device's dp index; one device sends to exactly 4 holder sections, exactly 8 blocks to each; each holder device receives at most 48 blocks from all sections, and in every dp column some holder receives exactly 48.
All inputs are finite; a program needn't handle non-finite values.
Results may differ from the reference program's by a relative error of at most 0.012.
Values may be sent and summed in bfloat16 or wider, within the bound.
A program may use at most 320 MiB of HBM per device.

```python
import math
import jax
import jax.numpy as jnp
from jax import lax

D = 8192
HID = 4096
TOK_DEV = 512
BLOCK = 128
SECTIONS = 8
DP_RANKS = 4
HID_SHARD = 512
TOKENS = 2048
ROW_BLOCKS = 16
SEND_MOST = 8
CAP = 48


def draw_holder_map(key, part):
    per_source = 2 * ROW_BLOCKS
    light_count = SECTIONS // 2
    order_key, block_key = jax.random.split(key)
    column_keys = jax.random.split(order_key, DP_RANKS)
    ranking = jax.vmap(lambda subkey: jax.random.permutation(subkey, SECTIONS))(column_keys)
    lighter = ranking[:, :light_count]
    heavier = ranking[:, light_count:]
    window = jnp.arange(SECTIONS) % light_count
    offsets = jnp.arange(1, light_count)
    light_entries = lighter[:, (window[:, None] + offsets[None, :]) % light_count]
    heavy_entry = heavier[:, window][:, :, None]
    entries = jnp.concatenate([light_entries, heavy_entry], axis=2)
    source_keys = jax.random.split(block_key, DP_RANKS * SECTIONS)
    shuffles = jax.vmap(lambda subkey: jax.random.permutation(subkey, per_source))(source_keys)
    group_of = shuffles.reshape(DP_RANKS, SECTIONS, per_source) // SEND_MOST
    holder = jnp.take_along_axis(entries, group_of, axis=2)
    holder = holder.reshape(DP_RANKS, SECTIONS, ROW_BLOCKS, 2).transpose(0, 2, 1, 3)
    return holder.reshape(DP_RANKS * ROW_BLOCKS, SECTIONS, 2).astype(jnp.int32)


def strengthened(drawn, own_key, source, target, shards_of, factor):
    def block_of(axis_at):
        return (jnp.arange(drawn.shape[axis_at]) // (drawn.shape[axis_at] // shards_of)).reshape((-1,) + (1,) * (drawn.ndim - 1 - axis_at))

    first = jax.random.permutation(own_key, shards_of)[block_of(target)]
    second = (block_of(target) + shards_of // 2) % shards_of
    return jnp.where((block_of(source) == first) | (block_of(source) == second), factor * drawn, drawn)


def shard_levels(rng, dims, pieces, low, top_value):
    def one(position, parts):
        heights = jax.random.uniform(jax.random.fold_in(jax.random.fold_in(rng, 6), position), (parts,), jnp.float32, low / len(pieces), top_value / len(pieces))
        return jnp.repeat(jnp.exp(heights), dims[position] // parts).reshape((-1,) + (1,) * (len(dims) - position - 1))

    loudness = one(*pieces[0])
    for cut in pieces[1:]:
        loudness = loudness * one(*cut)
    return loudness


def scatter_about(key, shape, spread, bound, cuts=(), held_as=jnp.bfloat16):
    loudness = shard_levels(key, shape, cuts, -0.22, 0.18) if cuts else 1.0
    drawn = jax.random.normal(key, shape, jnp.float32) * spread * loudness
    return jnp.minimum(jnp.maximum(drawn, -bound), bound).astype(held_as)


def bell_draw_with(own_key, extent, scale, reach, pieces, heavy, held_as=jnp.bfloat16):
    array = scale * jax.random.normal(own_key, extent, jnp.float32)
    if pieces:
        array = array * shard_levels(own_key, extent, pieces, -0.22, 0.18)
    return jnp.clip(strengthened(array, jax.random.fold_in(own_key, 3), *heavy), -reach, reach).astype(held_as)


def setup_inputs(seed: int = 0) -> dict:
    key_list = jax.random.split(jax.random.key(seed), 10)
    return {
        "activations": bell_draw_with(key_list[0], (TOKENS, D), 1.0, 6.0, ((0, 4),), (0, 1, 4, 2.0)),
        "cotangent": scatter_about(key_list[1], (TOKENS, D), 1.0, 6.0, ((0, 4),)),
        "gate_pre": scatter_about(key_list[2], (TOKENS, HID), 1.5, 6.0, ((0, 4), (1, 8))),
        "weights": scatter_about(key_list[3], (2, D, HID), D ** -0.5, 0.0625, ((1, 4), (2, 8))),
        "holder_map": draw_holder_map(jax.random.fold_in(key_list[9], 71), 0),
        "master": scatter_about(key_list[5], (SECTIONS, DP_RANKS, CAP, BLOCK, HID_SHARD), D ** -0.5, 0.0625, ((0, 8), (1, 4)), jnp.float32),
        "moment_one": scatter_about(key_list[6], (SECTIONS, DP_RANKS, CAP, BLOCK, HID_SHARD), (TOKENS ** 0.5 * 0.3), 80.0, ((0, 8), (1, 4)), jnp.float32),
        "moment_two": jnp.clip(jnp.exp(math.log(4096.0) - 3.6888794 * jax.random.uniform(key_list[7], (SECTIONS, DP_RANKS, CAP, BLOCK, HID_SHARD), jnp.float32) ** shard_levels(key_list[7], (SECTIONS, DP_RANKS, CAP, BLOCK, HID_SHARD), ((0, 8), (1, 4)), -0.2, 0.2)), 102.4, 4096.0),
        "adam_step": jax.random.randint(key_list[8], (1,), 1, 12).astype(jnp.int32),
    }


learn_rate = 0.03
beta_one = 0.9
beta_two = 0.95
adam_eps = 1e-08
decay_rate = 0.1

def adam_apply(gradient, weight_master, first_moment, second_moment, step_number):
    step_float = step_number.astype(jnp.float32)
    fix_one = 1.0 - jnp.power(jnp.float32(beta_one), step_float)
    fix_two = 1.0 - jnp.power(jnp.float32(beta_two), step_float)
    first_new = beta_one * first_moment + (1.0 - beta_one) * gradient
    second_new = beta_two * second_moment + (1.0 - beta_two) * gradient * gradient
    update = first_new / fix_one / (jnp.sqrt(second_new / fix_two) + adam_eps)
    return (weight_master * (1.0 - learn_rate * decay_rate) - learn_rate * update).astype(jnp.bfloat16)

def reference(activations, cotangent, gate_pre, weights, holder_map, master, moment_one, moment_two, adam_step):
    up_full = weights[0]
    down_full = weights[1]
    lifted = jnp.dot(activations, up_full, preferred_element_type=jnp.float32)
    back_hidden = jnp.dot(cotangent, down_full, preferred_element_type=jnp.float32)
    gate_silu = jax.nn.silu(gate_pre.astype(jnp.float32))
    hidden = (gate_silu * lifted).astype(jnp.bfloat16)
    back_up = (back_hidden * gate_silu).astype(jnp.bfloat16)
    up_groups = up_full.reshape(D, SECTIONS, HID_SHARD).transpose(1, 0, 2)
    back_groups = back_up.reshape(TOKENS, SECTIONS, HID_SHARD).transpose(1, 0, 2)

    def add_section(running, pair):
        part_up, part_back = pair
        term = lax.dot_general(part_back, part_up, (((1,), (1,)), ((), ())), preferred_element_type=jnp.float32)
        rounded = lax.optimization_barrier(term.astype(jnp.bfloat16))
        return (running + rounded.astype(jnp.float32), None)
    total_in, unused_in = lax.scan(add_section, jnp.zeros((TOKENS, D), jnp.float32), (up_groups, back_groups))
    passed_back = total_in.astype(jnp.bfloat16)

    def add_group(running, group):
        group_in, group_out, group_up, group_hidden = group
        term = jnp.stack([lax.dot_general(group_in, group_up, (((0,), (0,)), ((), ())), preferred_element_type=jnp.float32), lax.dot_general(group_out, group_hidden, (((0,), (0,)), ((), ())), preferred_element_type=jnp.float32)], axis=0)
        rounded = lax.optimization_barrier(term.astype(jnp.bfloat16))
        return (running + rounded.astype(jnp.float32), None)
    groups = (activations.reshape(DP_RANKS, TOK_DEV, D), cotangent.reshape(DP_RANKS, TOK_DEV, D), back_up.reshape(DP_RANKS, TOK_DEV, HID), hidden.reshape(DP_RANKS, TOK_DEV, HID))
    summed, unused = lax.scan(add_group, jnp.zeros((2, D, HID), jnp.float32), groups)
    total_blocks = D // BLOCK
    per_source = 2 * ROW_BLOCKS
    by_column = holder_map.reshape(DP_RANKS, ROW_BLOCKS, SECTIONS, 2).transpose(0, 2, 1, 3).reshape(DP_RANKS, SECTIONS * per_source)
    one_hot = (by_column[:, :, None] == jnp.arange(SECTIONS, dtype=jnp.int32)[None, None, :]).astype(jnp.int32)
    ahead = jnp.cumsum(one_hot, axis=1) - one_hot
    order_in = lax.optimization_barrier(jnp.sum(ahead * one_hot, axis=2)).astype(jnp.int32)
    slot_of = order_in.reshape(DP_RANKS, SECTIONS, ROW_BLOCKS, 2).transpose(0, 2, 1, 3).reshape(total_blocks, SECTIONS, 2)
    column_of = (jnp.arange(total_blocks, dtype=jnp.int32) // ROW_BLOCKS).astype(jnp.int32)[:, None, None]
    column_of = jnp.broadcast_to(column_of, holder_map.shape)
    grad_blocks = summed.reshape(2, total_blocks, BLOCK, SECTIONS, HID_SHARD).transpose(1, 3, 0, 2, 4)
    weight_master = master[holder_map, column_of, slot_of]
    first_moment = moment_one[holder_map, column_of, slot_of]
    second_moment = moment_two[holder_map, column_of, slot_of]
    updated = adam_apply(grad_blocks, weight_master, first_moment, second_moment, adam_step[0])
    new_weights = updated.transpose(2, 0, 3, 1, 4).reshape(2, D, HID)
    return (passed_back, new_weights)
```

```python
import jax
import jax.numpy as jnp
from jax import lax
from jax.experimental import pallas as pl
from jax.experimental.pallas import tpu as pltpu
from jax.sharding import PartitionSpec as P

learn_rate = 0.03
beta_one = 0.9
beta_two = 0.95
adam_eps = 1e-08
decay_rate = 0.1

BF16 = jnp.bfloat16
F32 = jnp.float32


COLS = 128
VMEM_BYTES = 62 * 2**20
MESH = pl.DeviceIdType.MESH


def spread_kernel(shape, cot_ref, act_ref, cot_out, act_out, held, local_sem, send_sem, recv_sem):
    sections, ranks, tok_dev, cols = shape
    chips = sections // 2
    piece = tok_dev // sections
    s = lax.axis_index("section")
    k = lax.axis_index("dp")
    core = lax.rem(s, 2)
    chip = s // 2
    sibling = (s + 1 - 2 * core, k)
    along = {d: (s, lax.rem(k + d, ranks)) for d in range(1, ranks)}
    across = {j: (2 * lax.rem(chip + j, chips) + core, k) for j in range(1, chips)}

    barrier = pltpu.get_barrier_semaphore()
    greeted = list(along.values()) + list(across.values()) + [sibling]
    for peer in greeted:
        pl.semaphore_signal(barrier, inc=1, device_id=peer, device_id_type=MESH)
    pl.semaphore_wait(barrier, len(greeted))

    pairs = ((cot_ref, cot_out), (act_ref, act_out))
    sems = iter(range(send_sem.shape[0]))

    def send(src, dst, peer):
        at = next(sems)
        copy = pltpu.make_async_remote_copy(
            src_ref=src,
            dst_ref=dst,
            send_sem=send_sem.at[at],
            recv_sem=recv_sem.at[at],
            device_id=peer,
            device_id_type=MESH,
        )
        copy.start()
        return copy

    def rows(out, rank, section):
        start = pl.multiple_of(rank * tok_dev + section * piece, piece)
        return out.at[pl.ds(start, piece), :]

    hops = {}
    for d in range(1, ranks):
        for a, (ref, out) in enumerate(pairs):
            start = pl.multiple_of(along[d][1] * cols, cols)
            from_rows = pl.ds(pl.multiple_of(s * piece, piece), piece)
            hops[a, d] = send(ref.at[from_rows, pl.ds(start, cols)], rows(out, k, s), along[d])
    own_cols = pl.ds(pl.multiple_of(k * cols, cols), cols)
    own_rows = pl.ds(pl.multiple_of(k * tok_dev, tok_dev), tok_dev)
    local = []
    for a, (ref, out) in enumerate(pairs):
        copy = pltpu.make_async_copy(ref.at[:, own_cols], held.at[a], local_sem.at[a])
        copy.start()
        local.append(copy)
    for a, (ref, out) in enumerate(pairs):
        local[a].wait()
        local[a] = pltpu.make_async_copy(held.at[a], out.at[own_rows, :], local_sem.at[2 + a])
        local[a].start()
    wide, last = {}, []
    for d in range(1, ranks):
        origin = lax.rem(k + ranks - d, ranks)
        for a, (ref, out) in enumerate(pairs):
            hops[a, d].wait_recv()
            block = rows(out, origin, s)
            for j in range(1, chips):
                wide[a, d, j] = send(block, block, across[j])
            last.append(send(block, block, sibling))
    for d in range(1, ranks):
        origin = lax.rem(k + ranks - d, ranks)
        for a, (ref, out) in enumerate(pairs):
            for j in range(1, chips):
                wide[a, d, j].wait_recv()
                block = rows(out, origin, 2 * lax.rem(chip + chips - j, chips) + core)
                last.append(send(block, block, sibling))
    for copy in last:
        copy.wait_recv()
    for copy in list(hops.values()) + list(wide.values()) + last:
        copy.wait_send()
    for copy in local:
        copy.wait()


def spread(cotangent, activations, sections, ranks):
    tok_dev, width = activations.shape
    cols = width // ranks
    copies = 2 * (ranks - 1) * sections
    out = jax.ShapeDtypeStruct((ranks * tok_dev, cols), activations.dtype)
    anywhere = pl.BlockSpec(memory_space=pl.ANY)
    moved = 2 * ranks * tok_dev * cols * 2

    def body(*refs):
        spread_kernel((sections, ranks, tok_dev, cols), *refs)

    return pl.pallas_call(
        body,
        out_shape=(out, out),
        in_specs=[anywhere, anywhere],
        out_specs=(anywhere, anywhere),
        scratch_shapes=[
            pltpu.VMEM((2, tok_dev, cols), activations.dtype),
            pltpu.SemaphoreType.DMA((4,)),
            pltpu.SemaphoreType.DMA((copies,)),
            pltpu.SemaphoreType.DMA((copies,)),
        ],
        compiler_params=pltpu.CompilerParams(collective_id=1, has_side_effects=True),
        cost_estimate=pl.CostEstimate(flops=0, bytes_accessed=8 * moved, transcendentals=0),
        name="spread",
    )(cotangent, activations)


class Pair:
    def __init__(self, src, dst, send_sem, recv_sem, peer):
        self.copy = pltpu.make_async_remote_copy(
            src_ref=src,
            dst_ref=dst,
            send_sem=send_sem,
            recv_sem=recv_sem,
            device_id=peer,
            device_id_type=MESH,
        )

    def start(self):
        self.copy.start()
        return self.copy


def layer_kernel(
    shape,
    pick_ref,
    place_ref,
    source_ref,
    rank_ref,
    fix_ref,
    act_hbm,
    cot_hbm,
    w_hbm,
    gate_hbm,
    master_hbm,
    first_hbm,
    second_hbm,
    back_out,
    new_out,
    act,
    cot,
    w,
    gate,
    part,
    landed,
    gathered,
    grads,
    outgoing,
    arrivals_even,
    arrivals_odd,
    updated,
    answers,
    returned_even,
    returned_odd,
    st_w,
    st_a,
    st_b,
    stage,
    from_sibling,
    from_chips,
    load_sem,
    state_sem,
    local_sem,
    place_sem,
    rs_send,
    rs_recv,
    ag_send,
    ag_recv,
    out_send,
    out_recv,
    ret_send,
    ret_recv,
    sib_send,
    sib_recv,
    chip_send,
    chip_recv,
    last_send,
    last_recv,
):
    sections, ranks, tok, units, row_count, rows, per_dest, groups = shape
    arrivals = (arrivals_even, arrivals_odd)
    returned = (returned_even, returned_odd)
    chunks = units // COLS
    chips = sections // 2
    split = sections // ranks
    depth = row_count // split
    row_blocks = row_count // rows
    per_row = row_count // tok
    s = lax.axis_index("section")
    k = lax.axis_index("dp")
    core = lax.rem(s, 2)
    chip = s // 2
    sibling = (s + 1 - 2 * core, k)
    along = [(s, lax.rem(k + d, ranks)) for d in range(ranks)]
    plane = [(lax.rem(s + e, sections), k) for e in range(sections)]
    across = [(2 * lax.rem(chip + j, chips) + core, k) for j in range(chips)]
    group_here = lax.rem(s // split + k, ranks)
    target_section = split * k + lax.rem(s, split)
    group_back = lax.rem(k + ranks - s // split, ranks)
    origin = (split * group_back + lax.rem(s, split), s // split)
    stays = (target_section == s) & (group_here == k)

    loads = []

    def load(src, dst):
        copy = pltpu.make_async_copy(src, dst, load_sem.at[len(loads)])
        copy.start()
        loads.append(copy)

    load(w_hbm, w)
    for d in range(ranks):
        t_rows = pl.ds(pl.multiple_of(along[d][1] * tok, tok), tok)
        load(cot_hbm.at[t_rows, :], cot.at[t_rows, :])
        load(act_hbm.at[t_rows, :], act.at[t_rows, :])
    load(gate_hbm, gate)

    def states_of(c):
        at = pl.ds(c * COLS, COLS)
        return [
            pltpu.make_async_copy(src.at[:, :, at], dst, state_sem.at[i])
            for i, (src, dst) in enumerate(
                ((master_hbm, st_w), (first_hbm, st_a), (second_hbm, st_b))
            )
        ]

    barrier = pltpu.get_barrier_semaphore()
    greeted = along[1:] + plane[1:]
    for peer in greeted:
        pl.semaphore_signal(barrier, inc=1, device_id=peer, device_id_type=MESH)

    @pl.when(jnp.logical_not(stays))
    def _():
        for peer in ((target_section, group_here), origin):
            pl.semaphore_signal(barrier, inc=1, device_id=peer, device_id_type=MESH)

    pl.semaphore_wait(barrier, jnp.where(stays, len(greeted), len(greeted) + 2))
    for copy in loads:
        copy.wait()
    for copy in states_of(0):
        copy.start()

    def lifted(c):
        at = slice(c * COLS, (c + 1) * COLS)

        def one(d, carry):
            t_rows = pl.ds(pl.multiple_of(lax.rem(k + d, ranks) * tok, tok), tok)
            part[d, :, :COLS] = jnp.dot(
                cot[t_rows, :], w[1, :, at], preferred_element_type=F32
            ).astype(BF16)
            part[d, :, COLS:] = jnp.dot(
                act[t_rows, :], w[0, :, at], preferred_element_type=F32
            ).astype(BF16)
            return carry

        lax.fori_loop(0, ranks, one, 0)

    def spread_sums():
        return [
            Pair(
                part.at[d], landed.at[d - 1], rs_send.at[d - 1], rs_recv.at[d - 1], along[d]
            ).start()
            for d in range(1, ranks)
        ]

    def gated(c):
        at = slice(c * COLS, (c + 1) * COLS)
        g = gate[:, at].astype(F32)
        silu = g / (1.0 + jnp.exp(-g))
        for m in range(2):
            cols = slice(m * COLS, (m + 1) * COLS)
            total = part[0, :, cols].astype(F32)
            for d in range(1, ranks):
                total += landed[d - 1, :, cols].astype(F32)
            gathered[k, m, at, :] = (total * silu).T.astype(BF16)

    def gather(c):
        at = pl.ds(c * COLS, COLS)
        block = gathered.at[k, :, at, :]
        return [
            Pair(block, block, ag_send.at[d - 1], ag_recv.at[d - 1], along[d]).start()
            for d in range(1, ranks)
        ]

    def gradients(c):
        at = slice(c * COLS, (c + 1) * COLS)
        tile = 2 * rows

        def one(j, carry):
            cols = pl.ds(pl.multiple_of(j * tile, tile), tile)
            for m, ref in enumerate((act, cot)):
                total = jnp.zeros((COLS, tile), F32)
                for t in range(ranks):
                    total += jnp.dot(
                        gathered[t, m, at, :],
                        ref[t * tok : (t + 1) * tok, cols],
                        preferred_element_type=F32,
                    )
                for b in range(2):
                    block = total[:, b * rows : (b + 1) * rows]
                    grads[m * row_blocks + 2 * j + b] = block.T.astype(BF16)
            return carry

        lax.fori_loop(0, row_blocks // 2, one, 0)

        def pick(q, carry):
            outgoing[q] = grads[pick_ref[q]]
            return carry

        lax.fori_loop(0, sections * per_dest, pick, 0)

    def slots(ref, section):
        return ref.at[pl.ds(section * per_dest, per_dest)]

    def exchange(src, dst, sends, recvs, c):
        copies = [
            Pair(
                slots(src, plane[e][0]),
                slots(dst[c % 2], s),
                sends.at[e - 1],
                recvs.at[c % 2, e - 1],
                plane[e],
            ).start()
            for e in range(1, sections)
        ]
        own = pltpu.make_async_copy(slots(src, s), slots(dst[c % 2], s), local_sem.at[0])
        own.start()
        own.wait()
        return copies

    def adam(c):
        scale_one = learn_rate / fix_ref[0]
        scale_two = 1.0 / fix_ref[1]
        arrived = arrivals[c % 2]

        def group(g, carry):
            base = source_ref[g] * per_dest

            def one(i, inner):
                at = g * per_dest + i
                grad = arrived[base + i].astype(F32)
                first = beta_one * st_a[at] + (1.0 - beta_one) * grad
                second = beta_two * st_b[at] + (1.0 - beta_two) * grad * grad
                update = (first * scale_one) / (jnp.sqrt(second * scale_two) + adam_eps)
                updated[at] = (st_w[at] * (1.0 - learn_rate * decay_rate) - update).astype(BF16)
                return inner

            return lax.fori_loop(0, per_dest, one, carry)

        lax.fori_loop(0, groups, group, 0)

    def answer():
        def one(d, carry):
            base = rank_ref[d] * per_dest

            def inner_one(i, inner):
                answers[d * per_dest + i] = updated[base + i]
                return inner

            return lax.fori_loop(0, per_dest, inner_one, carry)

        lax.fori_loop(0, sections, one, 0)

    def placed(c):
        source = returned[c % 2]

        def one(b, carry):
            stage[b] = source[place_ref[b]]
            return carry

        lax.fori_loop(0, 2 * row_blocks, one, 0)
        copy = pltpu.make_async_copy(
            stage, new_out.at[:, :, pl.ds(c * COLS, COLS)], place_sem.at[0]
        )
        copy.start()
        return copy

    def piece_at(ref, i):
        return ref.at[
            pl.ds((i // per_row) * depth, depth), pl.ds((i % per_row) * tok, tok)
        ]

    strip = 256

    def cotangent_piece(ref, i, owner, landed_ref):
        t = lax.rem(owner // split + k, ranks)
        half = lax.rem(owner, split)

        def one(r, carry):
            from_rows = pl.ds(pl.multiple_of(half * depth + r * strip, strip), strip)
            total = jnp.dot(w[0, from_rows, :], gathered[t, 0], preferred_element_type=F32)
            here = pl.ds(pl.multiple_of(r * strip, strip), strip)
            if landed_ref is not None:
                total += landed_ref[i, here, :].astype(F32)
            piece_at(ref, i)[here, :] = total.astype(BF16)
            return carry

        lax.fori_loop(0, depth // strip, one, 0)

    lifted(0)
    rs = spread_sums()
    gathers, outs, rets, places = {}, {}, {}, {}

    def returning(c):
        for copy in outs[c]:
            copy.wait_recv()
        for copy in states_of(c):
            copy.wait()
        adam(c)
        if c + 1 < chunks:
            for copy in states_of(c + 1):
                copy.start()
        if c > 0:
            for copy in rets[c - 1]:
                copy.wait_send()
        answer()
        rets[c] = exchange(answers, returned, ret_send, ret_recv, c)

    def placing(c):
        for copy in rets[c]:
            copy.wait_recv()
        if c > 0:
            places[c - 1].wait()
        places[c] = placed(c)

    for c in range(chunks):
        for copy in rs:
            copy.wait_recv()
        gated(c)
        if c > 0:
            for copy in gathers[c - 1]:
                copy.wait_send()
        gathers[c] = gather(c)
        for copy in rs:
            copy.wait_send()
        if c + 1 < chunks:
            lifted(c + 1)
        if c > 1:
            placing(c - 2)
        if c > 0:
            returning(c - 1)
        for copy in gathers[c]:
            copy.wait_recv()
        if c + 1 < chunks:
            rs = spread_sums()
        if c > 0:
            for copy in outs[c - 1]:
                copy.wait_send()
        gradients(c)
        outs[c] = exchange(outgoing, arrivals, out_send, out_recv, c)

    to_sibling = []
    for j in range(chips):
        cotangent_piece(act, j, 2 * lax.rem(chip + j, chips) + 1 - core, None)
        there = lax.rem(chip + j, chips)
        to_sibling.append(
            Pair(
                piece_at(act, j), from_sibling.at[j], sib_send.at[j], sib_recv.at[j], sibling
            ).start()
        )
    to_chips = []
    for j in list(range(1, chips)) + [0]:
        to_sibling[j].wait_recv()
        cotangent_piece(cot, j, across[j][0], from_sibling)
        if j > 0:
            to_chips.append(
                Pair(
                    piece_at(cot, j),
                    from_chips.at[j - 1],
                    chip_send.at[j - 1],
                    chip_recv.at[j - 1],
                    across[j],
                ).start()
            )
    if chunks > 1:
        placing(chunks - 2)
    returning(chunks - 1)
    for copy in to_chips:
        copy.wait_recv()
    for copy in to_sibling:
        copy.wait_send()
    result = act.at[pl.ds((ranks - 1) * tok, tok), pl.ds(0, depth)]

    def total_of(r):
        here = pl.ds(r * strip, strip)
        total = piece_at(cot, 0)[here, :].astype(F32)
        for j in range(1, chips):
            total += from_chips[j - 1, here, :].astype(F32)
        return total.T.astype(BF16)

    for r in range(depth // strip):
        result[:, r * strip : (r + 1) * strip] = total_of(r)
    last = Pair(
        result, back_out, last_send.at[0], last_recv.at[0], (target_section, group_here)
    )
    kept = pltpu.make_async_copy(result, back_out, local_sem.at[1])

    @pl.when(jnp.logical_not(stays))
    def _():
        last.start()

    @pl.when(stays)
    def _():
        kept.start()

    placing(chunks - 1)

    @pl.when(jnp.logical_not(stays))
    def _():
        last.copy.wait()

    @pl.when(stays)
    def _():
        kept.wait()

    for copies in (gathers[chunks - 1], outs[chunks - 1], rets[chunks - 1], to_chips):
        for copy in copies:
            copy.wait_send()
    places[chunks - 1].wait()


def layer(
    tables, act_full, cot_full, weights, gate_pre, states, sections, ranks, per_dest
):
    tokens, row_count = act_full.shape
    tok, units = gate_pre.shape
    capacity, rows = states[0].shape[:2]
    groups = capacity // per_dest
    chips = sections // 2
    depth = row_count * ranks // sections
    blocks = 2 * row_count // rows
    slots = sections * per_dest
    anywhere = pl.BlockSpec(memory_space=pl.ANY)
    scalars = pl.BlockSpec(memory_space=pltpu.SMEM)
    shape = (sections, ranks, tok, units, row_count, rows, per_dest, groups)

    def body(*refs):
        layer_kernel(shape, *refs)

    sems = pltpu.SemaphoreType.DMA
    flops = 2 * tokens * row_count * units * 5
    return pl.pallas_call(
        body,
        out_shape=(
            jax.ShapeDtypeStruct((tok, depth), BF16),
            jax.ShapeDtypeStruct((blocks, rows, units), BF16),
        ),
        in_specs=[scalars] * 5 + [anywhere] * 7,
        out_specs=(anywhere, anywhere),
        scratch_shapes=[
            pltpu.VMEM((tokens, row_count), BF16),
            pltpu.VMEM((tokens, row_count), BF16),
            pltpu.VMEM(weights.shape, BF16),
            pltpu.VMEM((tok, units), BF16),
            pltpu.VMEM((ranks, tok, 2 * COLS), BF16),
            pltpu.VMEM((ranks - 1, tok, 2 * COLS), BF16),
            pltpu.VMEM((ranks, 2, units, tok), BF16),
            pltpu.VMEM((blocks, rows, COLS), BF16),
            pltpu.VMEM((slots, rows, COLS), BF16),
            pltpu.VMEM((slots, rows, COLS), BF16),
            pltpu.VMEM((slots, rows, COLS), BF16),
            pltpu.VMEM((capacity, rows, COLS), BF16),
            pltpu.VMEM((slots, rows, COLS), BF16),
            pltpu.VMEM((slots, rows, COLS), BF16),
            pltpu.VMEM((slots, rows, COLS), BF16),
            pltpu.VMEM((capacity, rows, COLS), F32),
            pltpu.VMEM((capacity, rows, COLS), F32),
            pltpu.VMEM((capacity, rows, COLS), F32),
            pltpu.VMEM((blocks, rows, COLS), BF16),
            pltpu.VMEM((chips, depth, tok), BF16),
            pltpu.VMEM((chips - 1, depth, tok), BF16),
            sems((2 * ranks + 2,)),
            sems((3,)),
            sems((2,)),
            sems((1,)),
            sems((ranks - 1,)),
            sems((ranks - 1,)),
            sems((ranks - 1,)),
            sems((ranks - 1,)),
            sems((sections - 1,)),
            sems((2, sections - 1)),
            sems((sections - 1,)),
            sems((2, sections - 1)),
            sems((chips,)),
            sems((chips,)),
            sems((chips - 1,)),
            sems((chips - 1,)),
            sems((1,)),
            sems((1,)),
        ],
        compiler_params=pltpu.CompilerParams(
            collective_id=2, has_side_effects=True, vmem_limit_bytes=VMEM_BYTES
        ),
        cost_estimate=pl.CostEstimate(
            flops=flops, bytes_accessed=12 * capacity * rows * units, transcendentals=0
        ),
        name="layer",
    )(*tables, act_full, cot_full, weights, gate_pre, *states)


def per_device(
    activations, cotangent, gate_pre, weights, holder_map, master, moment_one, moment_two, adam_step
):
    sections = lax.axis_size("section")
    ranks = lax.axis_size("dp")
    here = lax.axis_index("section")
    row_count, hidden_units = weights.shape[1:]
    block_rows = master.shape[3]
    capacity = master.shape[2]
    row_blocks = row_count // block_rows
    per_dest = 4 * row_blocks // sections
    slots = sections * per_dest
    groups = capacity // per_dest

    owners = holder_map[:, 0, :].reshape(-1)
    section_ids = jnp.arange(sections, dtype=jnp.int32)
    choose = (owners[:, None] == section_ids[None, :]).astype(jnp.int32)
    totals = jnp.sum(choose, axis=0)
    every_total = lax.all_gather(totals, "section")
    every_total, activations, cotangent = lax.optimization_barrier(
        (every_total, activations, cotangent)
    )
    block_ids = jnp.arange(2 * row_blocks, dtype=jnp.int32)
    earlier = (owners[:, None] == owners[None, :]) & (block_ids[None, :] < block_ids[:, None])
    place = owners * per_dest + jnp.sum(earlier.astype(jnp.int32), axis=1)
    by_matrix = (block_ids % 2) * row_blocks + block_ids // 2
    pick = jnp.sum(
        jnp.where(
            place[None, :] == jnp.arange(slots, dtype=jnp.int32)[:, None], by_matrix[None, :], 0
        ),
        axis=1,
    )
    place = place.reshape(row_blocks, 2).T.reshape(-1)
    mine = jnp.sum(jnp.where(section_ids[None, :] == here, every_total, 0), axis=1)
    live = mine > 0
    rank_of = jnp.sum(
        (live[None, :] & (section_ids[None, :] < section_ids[:, None])).astype(jnp.int32), axis=1
    )
    wanted = jnp.arange(groups, dtype=jnp.int32)
    sources = jnp.sum(
        jnp.where(
            (rank_of[None, :] == wanted[:, None]) & live[None, :], section_ids[None, :], 0
        ),
        axis=1,
    )
    rank_of = jnp.minimum(rank_of, groups - 1)
    step_float = adam_step[0].astype(F32)
    fixes = jnp.stack(
        [
            1.0 - jnp.power(jnp.float32(beta_one), step_float),
            1.0 - jnp.power(jnp.float32(beta_two), step_float),
        ]
    )
    states = (master[0, 0], moment_one[0, 0], moment_two[0, 0])
    cot_full, act_full = spread(cotangent, activations, sections, ranks)
    passed_back, blocks = layer(
        (pick, place, sources, rank_of, fixes),
        act_full,
        cot_full,
        weights,
        gate_pre,
        states,
        sections,
        ranks,
        per_dest,
    )
    return (passed_back, blocks.reshape(weights.shape))


def solution(mesh):
    in_specs = (
        P("dp", None),
        P("dp", None),
        P("dp", "section"),
        P(None, "dp", "section"),
        P("dp", "section", None),
        P("section", "dp", None, None, None),
        P("section", "dp", None, None, None),
        P("section", "dp", None, None, None),
        P(),
    )
    out_specs = (P("dp", "section"), P(None, "dp", "section"))
    return jax.shard_map(
        per_device, mesh=mesh, in_specs=in_specs, out_specs=out_specs, check_vma=False
    )
```

```python
import jax
import jax.numpy as jnp
from jax import lax
from jax.experimental import pallas as pl
from jax.experimental.pallas import tpu as pltpu
from jax.sharding import PartitionSpec as P

learn_rate = 0.03
beta_one = 0.9
beta_two = 0.95
adam_eps = 1e-08
decay_rate = 0.1

BF16 = jnp.bfloat16
F32 = jnp.float32


COLS = 128
AHEAD = 2
VMEM_BYTES = 62 * 2**20
MESH = pl.DeviceIdType.MESH


class Pair:
    def __init__(self, src, dst, send_sem, recv_sem, peer):
        self.copy = pltpu.make_async_remote_copy(
            src_ref=src,
            dst_ref=dst,
            send_sem=send_sem,
            recv_sem=recv_sem,
            device_id=peer,
            device_id_type=MESH,
        )

    def start(self):
        self.copy.start()
        return self.copy


def layer_kernel(
    shape,
    pick_ref,
    place_ref,
    fix_ref,
    counts_hbm,
    act_hbm,
    cot_hbm,
    w_hbm,
    gate_hbm,
    master_hbm,
    first_hbm,
    second_hbm,
    back_out,
    new_out,
    act,
    cot,
    w,
    gate,
    part,
    landed,
    gathered,
    grads,
    outgoing,
    arrivals_even,
    arrivals_odd,
    updated,
    answers,
    returned_even,
    returned_odd,
    st_w,
    st_a,
    st_b,
    stage,
    from_sibling,
    from_chips,
    table,
    source_ref,
    rank_ref,
    load_sem,
    state_sem,
    local_sem,
    place_sem,
    count_send,
    count_recv,
    hop_send,
    hop_recv,
    wide_send,
    wide_recv,
    near_send,
    near_recv,
    rs_send,
    rs_recv,
    ag_send,
    ag_recv,
    out_send,
    out_recv,
    ret_send,
    ret_recv,
    sib_send,
    sib_recv,
    chip_send,
    chip_recv,
    last_send,
    last_recv,
    kept_sem,
):
    sections, ranks, tok, units, row_count, rows, per_dest, groups = shape
    arrivals = (arrivals_even, arrivals_odd)
    returned = (returned_even, returned_odd)
    chunks = units // COLS
    chips = sections // 2
    split = sections // ranks
    depth = row_count // split
    row_blocks = row_count // rows
    per_row = row_count // tok
    s = lax.axis_index("section")
    k = lax.axis_index("dp")
    core = lax.rem(s, 2)
    chip = s // 2
    sibling = (s + 1 - 2 * core, k)
    along = [(s, lax.rem(k + d, ranks)) for d in range(ranks)]
    plane = [(lax.rem(s + e, sections), k) for e in range(sections)]
    across = [(2 * lax.rem(chip + j, chips) + core, k) for j in range(chips)]
    if ranks == 4:

        def token_group(part, rank):
            low = lax.rem(rank // 2 + lax.rem(part, 2), 2)
            return 2 * lax.rem(lax.rem(rank, 2) + part // 2, 2) + low

        part_of = token_group
    else:

        def token_group(part, rank):
            return lax.rem(part + rank, ranks)

        def part_of(group, rank):
            return lax.rem(group + ranks - rank, ranks)

    group_here = token_group(s // split, k)
    target_section = split * k + lax.rem(s, split)
    group_back = part_of(k, s // split)
    origin = (split * group_back + lax.rem(s, split), s // split)
    stays = (target_section == s) & (group_here == k)

    loads = []

    def load(src, dst):
        copy = pltpu.make_async_copy(src, dst, load_sem.at[len(loads)])
        copy.start()
        loads.append(copy)

    own_cols = pl.ds(pl.multiple_of(k * row_count, row_count), row_count)
    own_rows = pl.ds(pl.multiple_of(k * tok, tok), tok)
    load(w_hbm, w)
    load(cot_hbm.at[:, own_cols], cot.at[own_rows, :])
    load(act_hbm.at[:, own_cols], act.at[own_rows, :])
    load(gate_hbm, gate)
    load(counts_hbm, table.at[s])

    def states_of(c):
        at = pl.ds(c * COLS, COLS)
        return [
            pltpu.make_async_copy(src.at[:, :, at], dst, state_sem.at[i])
            for i, (src, dst) in enumerate(
                ((master_hbm, st_w), (first_hbm, st_a), (second_hbm, st_b))
            )
        ]

    barrier = pltpu.get_barrier_semaphore()
    greeted = along[1:] + plane[1:]
    for peer in greeted:
        pl.semaphore_signal(barrier, inc=1, device_id=peer, device_id_type=MESH)

    @pl.when(jnp.logical_not(stays))
    def _():
        for peer in ((target_section, group_here), origin):
            pl.semaphore_signal(barrier, inc=1, device_id=peer, device_id_type=MESH)

    pl.semaphore_wait(barrier, jnp.where(stays, len(greeted), len(greeted) + 2))
    piece = tok // sections
    pairs = ((cot_hbm, cot), (act_hbm, act))
    folded = chips == 4
    if folded:
        chip_of = (chip, chip + 1 - 2 * lax.rem(chip, 2), lax.rem(chip + 2, 4), 3 - chip)
        reach = {kind: (2 * chip_of[kind] + core, k) for kind in (1, 2)}
    else:
        chip_of = [lax.rem(chip + chips - j, chips) for j in range(chips)]
        reach = {kind: across[kind] for kind in range(1, chips)}

    def block_of(a, d, kind):
        rank = lax.rem(k + ranks - d, ranks)
        start = pl.multiple_of(rank * tok + (2 * chip_of[kind] + core) * piece, piece)
        return pairs[a][1].at[pl.ds(start, piece), :]

    hops, wide, near = {}, {}, {}
    order = [
        (a, d)
        for d in sorted(range(1, ranks), key=lambda d: (min(d, ranks - d), d))
        for a in range(2)
    ]

    def go_hop(a, d):
        from_rows = pl.ds(pl.multiple_of(s * piece, piece), piece)
        cols = pl.ds(pl.multiple_of(along[d][1] * row_count, row_count), row_count)
        hops[a, d] = Pair(
            pairs[a][0].at[from_rows, cols],
            block_of(a, 0, 0),
            hop_send.at[a, d - 1],
            hop_recv.at[a, d - 1],
            along[d],
        ).start()

    for a, d in order[:AHEAD]:
        go_hop(a, d)
    counted = [
        Pair(
            counts_hbm, table.at[s], count_send.at[e - 1], count_recv.at[e - 1], plane[e]
        ).start()
        for e in range(1, sections)
    ]

    def go_wide(a, d, kind, block, peer):
        at = (a, d - 1, kind - 1)
        wide[a, d, kind] = Pair(block, block, wide_send.at[at], wide_recv.at[at], peer).start()

    def go_near(a, d, kind, block):
        at = (a, d - 1, kind)
        near[a, d, kind] = Pair(block, block, near_send.at[at], near_recv.at[at], sibling).start()

    def first_leg(a, d):
        block = block_of(a, d, 0)
        for kind, peer in reach.items():
            go_wide(a, d, kind, block, peer)
        go_near(a, d, 0, block)

    def second_leg(a, d):
        for kind in reach:
            wide[a, d, kind].wait_recv()
            block = block_of(a, d, kind)
            if folded and kind == 1 + a:
                go_wide(a, d, 3, block, reach[2 - a])
            go_near(a, d, kind, block)

    def third_leg(a, d):
        if folded:
            wide[a, d, 3].wait_recv()
            go_near(a, d, 3, block_of(a, d, 3))

    def group_done(d):
        for a in range(2):
            for kind in range(chips):
                near[a, d, kind].wait_recv()

    def lifted(c, first, last):
        at = slice(c * COLS, (c + 1) * COLS)

        def one(d, carry):
            t_rows = pl.ds(pl.multiple_of(lax.rem(k + d, ranks) * tok, tok), tok)
            part[d, :, :COLS] = jnp.dot(
                cot[t_rows, :], w[1, :, at], preferred_element_type=F32
            ).astype(BF16)
            part[d, :, COLS:] = jnp.dot(
                act[t_rows, :], w[0, :, at], preferred_element_type=F32
            ).astype(BF16)
            return carry

        lax.fori_loop(first, last, one, 0)

    def spread_sum(d):
        return Pair(
            part.at[d], landed.at[d - 1], rs_send.at[d - 1], rs_recv.at[d - 1], along[d]
        ).start()

    def spread_sums():
        return [spread_sum(d) for d in range(1, ranks)]

    def gated(c):
        at = slice(c * COLS, (c + 1) * COLS)
        g = gate[:, at].astype(F32)
        silu = g / (1.0 + jnp.exp(-g))
        for m in range(2):
            cols = slice(m * COLS, (m + 1) * COLS)
            total = part[0, :, cols].astype(F32)
            for d in range(1, ranks):
                total += landed[d - 1, :, cols].astype(F32)
            gathered[k, m, at, :] = (total * silu).T.astype(BF16)

    def gather(c):
        at = pl.ds(c * COLS, COLS)
        block = gathered.at[k, :, at, :]
        return [
            Pair(block, block, ag_send.at[d - 1], ag_recv.at[d - 1], along[d]).start()
            for d in range(1, ranks)
        ]

    def gradients(c):
        at = slice(c * COLS, (c + 1) * COLS)
        tile = 2 * rows

        def one(j, carry):
            cols = pl.ds(pl.multiple_of(j * tile, tile), tile)
            for m, ref in enumerate((act, cot)):
                total = jnp.zeros((COLS, tile), F32)
                for t in range(ranks):
                    total += jnp.dot(
                        gathered[t, m, at, :],
                        ref[t * tok : (t + 1) * tok, cols],
                        preferred_element_type=F32,
                    )
                for b in range(2):
                    block = total[:, b * rows : (b + 1) * rows]
                    grads[m * row_blocks + 2 * j + b] = block.T.astype(BF16)
            return carry

        lax.fori_loop(0, row_blocks // 2, one, 0)

        def pick(q, carry):
            outgoing[q] = grads[pick_ref[q]]
            return carry

        lax.fori_loop(0, sections * per_dest, pick, 0)

    def slots(ref, section):
        return ref.at[pl.ds(section * per_dest, per_dest)]

    def exchange(src, dst, sends, recvs, c):
        copies = [
            Pair(
                slots(src, plane[e][0]),
                slots(dst[c % 2], s),
                sends.at[e - 1],
                recvs.at[c % 2, e - 1],
                plane[e],
            ).start()
            for e in range(1, sections)
        ]
        own = pltpu.make_async_copy(slots(src, s), slots(dst[c % 2], s), local_sem.at[0])
        own.start()
        own.wait()
        return copies

    def ranking():
        lane = lax.broadcasted_iota(jnp.int32, (1, 128), 1)
        lives = [
            (jnp.sum(jnp.where(lane == s, table[p, 0:1, :], 0)) > 0).astype(jnp.int32)
            for p in range(sections)
        ]
        before = jnp.int32(0)
        sources = [jnp.int32(0)] * groups
        for p in range(sections):
            rank_ref[p] = jnp.minimum(before, groups - 1)
            for g in range(groups):
                sources[g] += jnp.where(before == g, lives[p] * p, 0)
            before += lives[p]
        for g in range(groups):
            source_ref[g] = sources[g]

    def adam(c):
        scale_one = learn_rate / fix_ref[0]
        scale_two = 1.0 / fix_ref[1]
        arrived = arrivals[c % 2]

        def group(g, carry):
            base = source_ref[g] * per_dest

            def one(i, inner):
                at = g * per_dest + i
                grad = arrived[base + i].astype(F32)
                first = beta_one * st_a[at] + (1.0 - beta_one) * grad
                second = beta_two * st_b[at] + (1.0 - beta_two) * grad * grad
                update = (first * scale_one) / (jnp.sqrt(second * scale_two) + adam_eps)
                updated[at] = (st_w[at] * (1.0 - learn_rate * decay_rate) - update).astype(BF16)
                return inner

            return lax.fori_loop(0, per_dest, one, carry)

        lax.fori_loop(0, groups, group, 0)

    def answer():
        def one(d, carry):
            base = rank_ref[d] * per_dest

            def inner_one(i, inner):
                answers[d * per_dest + i] = updated[base + i]
                return inner

            return lax.fori_loop(0, per_dest, inner_one, carry)

        lax.fori_loop(0, sections, one, 0)

    def placed(c):
        source = returned[c % 2]

        def one(b, carry):
            stage[b] = source[place_ref[b]]
            return carry

        lax.fori_loop(0, 2 * row_blocks, one, 0)
        copy = pltpu.make_async_copy(
            stage, new_out.at[:, :, pl.ds(c * COLS, COLS)], place_sem.at[0]
        )
        copy.start()
        return copy

    def piece_at(ref, i):
        return ref.at[
            pl.ds((i // per_row) * depth, depth), pl.ds((i % per_row) * tok, tok)
        ]

    strip = 256
    strips = depth // strip
    kind_chip = chip_of if folded else [lax.rem(chip + j, chips) for j in range(chips)]

    def strip_of(r):
        return pl.ds(pl.multiple_of(r * strip, strip), strip)

    def cotangent_strip(owner, r):
        t = token_group(owner // split, k)
        half = lax.rem(owner, split)
        start = pl.multiple_of(half * depth + r * strip, strip)
        return jnp.dot(
            w[0, pl.ds(start, strip), :], gathered[t, 0], preferred_element_type=F32
        )

    def kept_strip(j, r):
        owned = cotangent_strip(2 * kind_chip[j] + core, r)
        return owned + from_sibling[j, strip_of(r), :].astype(F32)

    def sibling_piece(j):
        def one(r, carry):
            total = cotangent_strip(2 * kind_chip[j] + 1 - core, r)
            piece_at(act, j)[strip_of(r), :] = total.astype(BF16)
            return carry

        lax.fori_loop(0, strips, one, 0)

    def strip_to(total, j, r, at, peer):
        here = strip_of(r)
        piece_at(cot, j)[here, :] = total.astype(BF16)
        return Pair(
            piece_at(cot, j).at[here, :],
            from_chips.at[at, here, :],
            chip_send.at[at, r],
            chip_recv.at[at, r],
            peer,
        ).start()

    rs = []
    for i in range(len(order) + 2):
        if i < len(order):
            hops[order[i]].wait_recv()
            if i + AHEAD < len(order):
                go_hop(*order[i + AHEAD])
            first_leg(*order[i])
        if 1 <= i <= len(order):
            second_leg(*order[i - 1])
        if i == 1:
            for copy in loads:
                copy.wait()
            for copy in states_of(0):
                copy.start()
            lifted(0, 0, 1)
        if i >= 2:
            third_leg(*order[i - 2])
            a, d = order[i - 2]
            if a == 1:
                group_done(d)
                lifted(0, ranks - d, ranks - d + 1)
                rs.append(spread_sum(ranks - d))
    for copies in (hops, wide, near):
        for copy in copies.values():
            copy.wait_send()
    for copy in counted:
        copy.wait()
    ranking()
    gathers, outs, rets, places = {}, {}, {}, {}

    def returning(c):
        for copy in outs[c]:
            copy.wait_recv()
        for copy in states_of(c):
            copy.wait()
        adam(c)
        if c + 1 < chunks:
            for copy in states_of(c + 1):
                copy.start()
        if c > 0:
            for copy in rets[c - 1]:
                copy.wait_send()
        answer()
        rets[c] = exchange(answers, returned, ret_send, ret_recv, c)

    def placing(c):
        for copy in rets[c]:
            copy.wait_recv()
        if c > 0:
            places[c - 1].wait()
        places[c] = placed(c)

    for c in range(chunks):
        for copy in rs:
            copy.wait_recv()
        gated(c)
        if c > 0:
            for copy in gathers[c - 1]:
                copy.wait_send()
        gathers[c] = gather(c)
        for copy in rs:
            copy.wait_send()
        if c + 1 < chunks:
            lifted(c + 1, 0, ranks)
        if c > 1:
            placing(c - 2)
        if c > 0:
            returning(c - 1)
        for copy in gathers[c]:
            copy.wait_recv()
        if c + 1 < chunks:
            rs = spread_sums()
        if c > 0:
            for copy in outs[c - 1]:
                copy.wait_send()
        gradients(c)
        if c + 1 < chunks:
            outs[c] = exchange(outgoing, arrivals, out_send, out_recv, c)

    to_sibling = []
    for j in list(range(1, chips)) + [0]:
        sibling_piece(j)
        to_sibling.append(
            Pair(
                piece_at(act, j), from_sibling.at[j], sib_send.at[j], sib_recv.at[j], sibling
            ).start()
        )
    for copy in to_sibling:
        copy.wait_recv()
    to_chips = {}
    for r in range(strips):
        if folded:
            near_kind = 1 + r % 2
            for at, j in enumerate((near_kind, 3)):
                to_chips[at, r] = strip_to(kept_strip(j, r), j, r, at, reach[near_kind])
        else:
            for j in range(1, chips):
                to_chips[j - 1, r] = strip_to(kept_strip(j, r), j, r, j - 1, across[j])
    if chunks > 1:
        placing(chunks - 2)
    if folded:
        for r in range(strips):
            far_kind = 2 - r % 2
            to_chips[1, r].wait_recv()
            total = kept_strip(far_kind, r) + from_chips[1, strip_of(r), :].astype(F32)
            to_chips[2, r] = strip_to(total, far_kind, r, 2, reach[far_kind])
    outs[chunks - 1] = exchange(outgoing, arrivals, out_send, out_recv, chunks - 1)
    returning(chunks - 1)
    for copy in to_sibling:
        copy.wait_send()
    result = act.at[pl.ds((ranks - 1) * tok, tok), pl.ds(0, depth)]
    lasts = []
    for r in range(strips):
        total = kept_strip(0, r)
        for j in range(chips - 1):
            if not (folded and j == 1):
                to_chips[j, r].wait_recv()
                total += from_chips[j, strip_of(r), :].astype(F32)
        result[:, r * strip : (r + 1) * strip] = total.T.astype(BF16)
        there = pl.ds(r * strip, strip)
        last = Pair(
            result.at[:, there],
            back_out.at[:, there],
            last_send.at[r],
            last_recv.at[r],
            (target_section, group_here),
        )
        kept = pltpu.make_async_copy(
            result.at[:, there], back_out.at[:, there], kept_sem.at[r]
        )
        lasts.append((last, kept))

        @pl.when(jnp.logical_not(stays))
        def _():
            last.start()

        @pl.when(stays)
        def _():
            kept.start()

    placing(chunks - 1)

    @pl.when(jnp.logical_not(stays))
    def _():
        for last, kept in lasts:
            last.copy.wait()

    @pl.when(stays)
    def _():
        for last, kept in lasts:
            kept.wait()

    for copy in to_chips.values():
        copy.wait_send()
    for copies in (gathers[chunks - 1], outs[chunks - 1], rets[chunks - 1]):
        for copy in copies:
            copy.wait_send()
    places[chunks - 1].wait()


def layer(tables, counts, activations, cotangent, weights, gate_pre, states, sections, ranks, per_dest):
    row_count = weights.shape[1]
    tok, units = gate_pre.shape
    tokens = tok * ranks
    capacity, rows = states[0].shape[:2]
    groups = capacity // per_dest
    chips = sections // 2
    depth = row_count * ranks // sections
    strips = depth // 256
    blocks = 2 * row_count // rows
    slots = sections * per_dest
    anywhere = pl.BlockSpec(memory_space=pl.ANY)
    scalars = pl.BlockSpec(memory_space=pltpu.SMEM)
    shape = (sections, ranks, tok, units, row_count, rows, per_dest, groups)

    def body(*refs):
        layer_kernel(shape, *refs)

    sems = pltpu.SemaphoreType.DMA
    flops = 2 * tokens * row_count * units * 5
    return pl.pallas_call(
        body,
        out_shape=(
            jax.ShapeDtypeStruct((tok, depth), BF16),
            jax.ShapeDtypeStruct((blocks, rows, units), BF16),
        ),
        in_specs=[scalars] * 3 + [anywhere] * 8,
        out_specs=(anywhere, anywhere),
        scratch_shapes=[
            pltpu.VMEM((tokens, row_count), BF16),
            pltpu.VMEM((tokens, row_count), BF16),
            pltpu.VMEM(weights.shape, BF16),
            pltpu.VMEM((tok, units), BF16),
            pltpu.VMEM((ranks, tok, 2 * COLS), BF16),
            pltpu.VMEM((ranks - 1, tok, 2 * COLS), BF16),
            pltpu.VMEM((ranks, 2, units, tok), BF16),
            pltpu.VMEM((blocks, rows, COLS), BF16),
            pltpu.VMEM((slots, rows, COLS), BF16),
            pltpu.VMEM((slots, rows, COLS), BF16),
            pltpu.VMEM((slots, rows, COLS), BF16),
            pltpu.VMEM((capacity, rows, COLS), BF16),
            pltpu.VMEM((slots, rows, COLS), BF16),
            pltpu.VMEM((slots, rows, COLS), BF16),
            pltpu.VMEM((slots, rows, COLS), BF16),
            pltpu.VMEM((capacity, rows, COLS), F32),
            pltpu.VMEM((capacity, rows, COLS), F32),
            pltpu.VMEM((capacity, rows, COLS), F32),
            pltpu.VMEM((blocks, rows, COLS), BF16),
            pltpu.VMEM((chips, depth, tok), BF16),
            pltpu.VMEM((chips - 1, depth, tok), BF16),
            pltpu.VMEM((sections, 8, 128), jnp.int32),
            pltpu.SMEM((groups,), jnp.int32),
            pltpu.SMEM((sections,), jnp.int32),
            sems((5,)),
            sems((3,)),
            sems((2,)),
            sems((1,)),
            sems((sections - 1,)),
            sems((sections - 1,)),
            sems((2, ranks - 1)),
            sems((2, ranks - 1)),
            sems((2, ranks - 1, chips - 1)),
            sems((2, ranks - 1, chips - 1)),
            sems((2, ranks - 1, chips)),
            sems((2, ranks - 1, chips)),
            sems((ranks - 1,)),
            sems((ranks - 1,)),
            sems((ranks - 1,)),
            sems((ranks - 1,)),
            sems((sections - 1,)),
            sems((2, sections - 1)),
            sems((sections - 1,)),
            sems((2, sections - 1)),
            sems((chips,)),
            sems((chips,)),
            sems((chips - 1, strips)),
            sems((chips - 1, strips)),
            sems((strips,)),
            sems((strips,)),
            sems((strips,)),
        ],
        compiler_params=pltpu.CompilerParams(
            collective_id=2, has_side_effects=True, vmem_limit_bytes=VMEM_BYTES
        ),
        cost_estimate=pl.CostEstimate(
            flops=flops, bytes_accessed=12 * capacity * rows * units, transcendentals=0
        ),
        name="layer",
    )(*tables, counts, activations, cotangent, weights, gate_pre, *states)


def per_device(
    activations, cotangent, gate_pre, weights, holder_map, master, moment_one, moment_two, adam_step
):
    sections = lax.axis_size("section")
    ranks = lax.axis_size("dp")
    row_count, hidden_units = weights.shape[1:]
    block_rows = master.shape[3]
    row_blocks = row_count // block_rows
    per_dest = 4 * row_blocks // sections
    slots = sections * per_dest

    owners = holder_map[:, 0, :].reshape(-1)
    section_ids = jnp.arange(sections, dtype=jnp.int32)
    choose = (owners[:, None] == section_ids[None, :]).astype(jnp.int32)
    counts = jnp.pad(jnp.sum(choose, axis=0)[None, :], ((0, 7), (0, 128 - sections)))
    block_ids = jnp.arange(2 * row_blocks, dtype=jnp.int32)
    earlier = (owners[:, None] == owners[None, :]) & (block_ids[None, :] < block_ids[:, None])
    place = owners * per_dest + jnp.sum(earlier.astype(jnp.int32), axis=1)
    by_matrix = (block_ids % 2) * row_blocks + block_ids // 2
    pick = jnp.sum(
        jnp.where(
            place[None, :] == jnp.arange(slots, dtype=jnp.int32)[:, None], by_matrix[None, :], 0
        ),
        axis=1,
    )
    place = place.reshape(row_blocks, 2).T.reshape(-1)
    step_float = adam_step[0].astype(F32)
    fixes = jnp.stack(
        [
            1.0 - jnp.power(jnp.float32(beta_one), step_float),
            1.0 - jnp.power(jnp.float32(beta_two), step_float),
        ]
    )
    states = (master[0, 0], moment_one[0, 0], moment_two[0, 0])
    passed_back, blocks = layer(
        (pick, place, fixes),
        counts,
        activations,
        cotangent,
        weights,
        gate_pre,
        states,
        sections,
        ranks,
        per_dest,
    )
    return (passed_back, blocks.reshape(weights.shape))


def solution(mesh):
    in_specs = (
        P("dp", None),
        P("dp", None),
        P("dp", "section"),
        P(None, "dp", "section"),
        P("dp", "section", None),
        P("section", "dp", None, None, None),
        P("section", "dp", None, None, None),
        P("section", "dp", None, None, None),
        P(),
    )
    out_specs = (P("dp", "section"), P(None, "dp", "section"))
    return jax.shard_map(
        per_device, mesh=mesh, in_specs=in_specs, out_specs=out_specs, check_vma=False
    )
```

```python
import math

import jax
import jax.numpy as jnp
from jax import lax
from jax.experimental import pallas as pl
from jax.experimental.pallas import tpu as pltpu
from jax.sharding import PartitionSpec as P

learn_rate = 0.03
beta_one = 0.9
beta_two = 0.95
adam_eps = 1e-08
decay_rate = 0.1

BF16 = jnp.bfloat16
F32 = jnp.float32


COLS = 128
AHEAD = 2
HALVES = 2
VMEM_BYTES = 62 * 2**20
MESH = pl.DeviceIdType.MESH


class Pair:
    def __init__(self, src, dst, send_sem, recv_sem, peer):
        self.copy = pltpu.make_async_remote_copy(
            src_ref=src,
            dst_ref=dst,
            send_sem=send_sem,
            recv_sem=recv_sem,
            device_id=peer,
            device_id_type=MESH,
        )

    def start(self):
        self.copy.start()
        return self.copy


def layer_kernel(
    shape,
    owner_ref,
    step_ref,
    act_hbm,
    cot_hbm,
    w_hbm,
    gate_hbm,
    master_hbm,
    first_hbm,
    second_hbm,
    back_out,
    new_out,
    act,
    cot,
    w,
    gate,
    part,
    landed,
    gathered,
    grads,
    outgoing,
    arrivals_even,
    arrivals_odd,
    updated,
    answers,
    returned_even,
    returned_odd,
    st_w,
    st_a,
    st_b,
    stage,
    from_sibling,
    from_chips,
    counts,
    table,
    pick_ref,
    place_ref,
    source_ref,
    rank_ref,
    load_sem,
    state_sem,
    local_sem,
    place_sem,
    count_send,
    count_recv,
    hop_send,
    hop_recv,
    wide_send,
    wide_recv,
    near_send,
    near_recv,
    rs_send,
    rs_recv,
    ag_send,
    ag_recv,
    out_send,
    out_recv,
    ret_send,
    ret_recv,
    sib_send,
    sib_recv,
    chip_send,
    chip_recv,
    last_send,
    last_recv,
    kept_sem,
):
    sections, ranks, tok, units, row_count, rows, per_dest, groups = shape
    arrivals = (arrivals_even, arrivals_odd)
    returned = (returned_even, returned_odd)
    chunks = units // COLS
    chips = sections // 2
    split = sections // ranks
    depth = row_count // split
    row_blocks = row_count // rows
    per_row = row_count // tok
    s = lax.axis_index("section")
    k = lax.axis_index("dp")
    core = lax.rem(s, 2)
    chip = s // 2
    sibling = (s + 1 - 2 * core, k)
    along = [(s, lax.rem(k + d, ranks)) for d in range(ranks)]
    plane = [(lax.rem(s + e, sections), k) for e in range(sections)]
    across = [(2 * lax.rem(chip + j, chips) + core, k) for j in range(chips)]
    if ranks == 4:

        def token_group(part, rank):
            low = lax.rem(rank // 2 + lax.rem(part, 2), 2)
            return 2 * lax.rem(lax.rem(rank, 2) + part // 2, 2) + low

        part_of = token_group
    else:

        def token_group(part, rank):
            return lax.rem(part + rank, ranks)

        def part_of(group, rank):
            return lax.rem(group + ranks - rank, ranks)

    group_here = token_group(s // split, k)
    target_section = split * k + lax.rem(s, split)
    group_back = part_of(k, s // split)
    origin = (split * group_back + lax.rem(s, split), s // split)
    stays = (target_section == s) & (group_here == k)

    loads = []

    def load(src, dst):
        copy = pltpu.make_async_copy(src, dst, load_sem.at[len(loads)])
        copy.start()
        loads.append(copy)

    own_cols = pl.ds(pl.multiple_of(k * row_count, row_count), row_count)
    own_rows = pl.ds(pl.multiple_of(k * tok, tok), tok)
    load(w_hbm, w)
    load(cot_hbm.at[:, own_cols], cot.at[own_rows, :])
    load(act_hbm.at[:, own_cols], act.at[own_rows, :])
    load(gate_hbm, gate)
    lanes = lax.broadcasted_iota(jnp.int32, counts.shape, 1)
    held = jnp.zeros(counts.shape, jnp.int32)
    for b in range(2 * row_blocks):
        held += (lanes == owner_ref[b]).astype(jnp.int32)
    counts[...] = held
    load(counts, table.at[s])

    def states_of(c):
        at = pl.ds(c * COLS, COLS)
        return [
            pltpu.make_async_copy(src.at[:, :, at], dst, state_sem.at[i])
            for i, (src, dst) in enumerate(
                ((master_hbm, st_w), (first_hbm, st_a), (second_hbm, st_b))
            )
        ]

    barrier = pltpu.get_barrier_semaphore()
    greeted = along[1:] + plane[1:]
    for peer in greeted:
        pl.semaphore_signal(barrier, inc=1, device_id=peer, device_id_type=MESH)

    @pl.when(jnp.logical_not(stays))
    def _():
        for peer in ((target_section, group_here), origin):
            pl.semaphore_signal(barrier, inc=1, device_id=peer, device_id_type=MESH)

    pl.semaphore_wait(barrier, jnp.where(stays, len(greeted), len(greeted) + 2))
    piece = tok // sections
    pairs = ((cot_hbm, cot), (act_hbm, act))
    folded = chips == 4
    if folded:
        chip_of = (chip, chip + 1 - 2 * lax.rem(chip, 2), lax.rem(chip + 2, 4), 3 - chip)
        reach = {kind: (2 * chip_of[kind] + core, k) for kind in (1, 2)}
    else:
        chip_of = [lax.rem(chip + chips - j, chips) for j in range(chips)]
        reach = {kind: across[kind] for kind in range(1, chips)}

    def block_of(a, d, kind):
        rank = lax.rem(k + ranks - d, ranks)
        start = pl.multiple_of(rank * tok + (2 * chip_of[kind] + core) * piece, piece)
        return pairs[a][1].at[pl.ds(start, piece), :]

    hops, wide, near = {}, {}, {}
    order = [
        (a, d)
        for d in sorted(range(1, ranks), key=lambda d: (min(d, ranks - d), d))
        for a in range(2)
    ]

    def go_hop(a, d):
        from_rows = pl.ds(pl.multiple_of(s * piece, piece), piece)
        cols = pl.ds(pl.multiple_of(along[d][1] * row_count, row_count), row_count)
        hops[a, d] = Pair(
            pairs[a][0].at[from_rows, cols],
            block_of(a, 0, 0),
            hop_send.at[a, d - 1],
            hop_recv.at[a, d - 1],
            along[d],
        ).start()

    for a, d in order[:AHEAD]:
        go_hop(a, d)
    counted = [
        Pair(
            counts, table.at[s], count_send.at[e - 1], count_recv.at[e - 1], plane[e]
        ).start()
        for e in range(1, sections)
    ]

    def go_wide(a, d, kind, block, peer):
        at = (a, d - 1, kind - 1)
        wide[a, d, kind] = Pair(block, block, wide_send.at[at], wide_recv.at[at], peer).start()

    def go_near(a, d, kind, block):
        at = (a, d - 1, kind)
        near[a, d, kind] = Pair(block, block, near_send.at[at], near_recv.at[at], sibling).start()

    def first_leg(a, d):
        block = block_of(a, d, 0)
        for kind, peer in reach.items():
            go_wide(a, d, kind, block, peer)
        go_near(a, d, 0, block)

    def second_leg(a, d):
        for kind in reach:
            wide[a, d, kind].wait_recv()
            block = block_of(a, d, kind)
            if folded and kind == 1 + a:
                go_wide(a, d, 3, block, reach[2 - a])
            go_near(a, d, kind, block)

    def third_leg(a, d):
        if folded:
            wide[a, d, 3].wait_recv()
            go_near(a, d, 3, block_of(a, d, 3))

    def group_done(d):
        for a in range(2):
            for kind in range(chips):
                near[a, d, kind].wait_recv()

    def lifted(c, first, last):
        at = slice(c * COLS, (c + 1) * COLS)

        def one(d, carry):
            t_rows = pl.ds(pl.multiple_of(lax.rem(k + d, ranks) * tok, tok), tok)
            part[d, :, :COLS] = jnp.dot(
                cot[t_rows, :], w[1, :, at], preferred_element_type=F32
            ).astype(BF16)
            part[d, :, COLS:] = jnp.dot(
                act[t_rows, :], w[0, :, at], preferred_element_type=F32
            ).astype(BF16)
            return carry

        lax.fori_loop(first, last, one, 0)

    half_tok = tok // HALVES

    def half_of(h):
        return slice(h * half_tok, (h + 1) * half_tok)

    def spread_sum(d, h):
        here = pl.ds(h * half_tok, half_tok)
        return Pair(
            part.at[d, here, :],
            landed.at[d - 1, here, :],
            rs_send.at[h, d - 1],
            rs_recv.at[h, d - 1],
            along[d],
        ).start()

    def gated(c, h):
        at = slice(c * COLS, (c + 1) * COLS)
        here = half_of(h)
        g = gate[here, at].astype(F32)
        silu = g / (1.0 + jnp.exp(-g))
        for m in range(2):
            cols = slice(m * COLS, (m + 1) * COLS)
            total = part[0, here, cols].astype(F32)
            for d in range(1, ranks):
                total += landed[d - 1, here, cols].astype(F32)
            gathered[k, m, at, here] = (total * silu).T.astype(BF16)

    def gather(c, h):
        block = gathered.at[k, :, pl.ds(c * COLS, COLS), pl.ds(h * half_tok, half_tok)]
        return [
            Pair(block, block, ag_send.at[h, d - 1], ag_recv.at[h, d - 1], along[d]).start()
            for d in range(1, ranks)
        ]

    def gradients(c):
        at = slice(c * COLS, (c + 1) * COLS)
        tile = 2 * rows

        def one(j, carry):
            cols = pl.ds(pl.multiple_of(j * tile, tile), tile)
            for m, ref in enumerate((act, cot)):
                total = jnp.zeros((COLS, tile), F32)
                for t in range(ranks):
                    total += jnp.dot(
                        gathered[t, m, at, :],
                        ref[t * tok : (t + 1) * tok, cols],
                        preferred_element_type=F32,
                    )
                for b in range(2):
                    block = total[:, b * rows : (b + 1) * rows]
                    grads[m * row_blocks + 2 * j + b] = block.T.astype(BF16)
            return carry

        lax.fori_loop(0, row_blocks // 2, one, 0)

        def pick(q, carry):
            outgoing[q] = grads[pick_ref[q]]
            return carry

        lax.fori_loop(0, sections * per_dest, pick, 0)

    def slots(ref, section):
        return ref.at[pl.ds(section * per_dest, per_dest)]

    def exchange(src, dst, sends, recvs, c):
        copies = [
            Pair(
                slots(src, plane[e][0]),
                slots(dst[c % 2], s),
                sends.at[e - 1],
                recvs.at[c % 2, e - 1],
                plane[e],
            ).start()
            for e in range(1, sections)
        ]
        own = pltpu.make_async_copy(slots(src, s), slots(dst[c % 2], s), local_sem.at[0])
        own.start()
        own.wait()
        return copies

    def places_of_blocks():
        count = 2 * row_blocks

        def one(b, carry):
            owner = owner_ref[b]
            order_in = jnp.int32(0)
            for other in range(count):
                order_in += jnp.where((owner_ref[other] == owner) & (other < b), 1, 0)
            place_ref[lax.rem(b, 2) * row_blocks + b // 2] = owner * per_dest + order_in
            return carry

        lax.fori_loop(0, count, one, 0)

        def back(q, carry):
            block = jnp.int32(0)
            for b in range(count):
                block += jnp.where(place_ref[b] == q, b, 0)
            pick_ref[q] = block
            return carry

        lax.fori_loop(0, sections * per_dest, back, 0)

    def ranking():
        lane = lax.broadcasted_iota(jnp.int32, (1, 128), 1)
        lives = [
            (jnp.sum(jnp.where(lane == s, table[p, 0:1, :], 0)) > 0).astype(jnp.int32)
            for p in range(sections)
        ]
        before = jnp.int32(0)
        sources = [jnp.int32(0)] * groups
        for p in range(sections):
            rank_ref[p] = jnp.minimum(before, groups - 1)
            for g in range(groups):
                sources[g] += jnp.where(before == g, lives[p] * p, 0)
            before += lives[p]
        for g in range(groups):
            source_ref[g] = sources[g]

    def adam(c):
        step = jnp.full((1, COLS), step_ref[0].astype(F32), F32)
        scale_one = learn_rate / (1.0 - jnp.exp(step * math.log(beta_one)))
        scale_two = 1.0 / (1.0 - jnp.exp(step * math.log(beta_two)))
        arrived = arrivals[c % 2]

        def group(g, carry):
            base = source_ref[g] * per_dest

            def one(i, inner):
                at = g * per_dest + i
                grad = arrived[base + i].astype(F32)
                first = beta_one * st_a[at] + (1.0 - beta_one) * grad
                second = beta_two * st_b[at] + (1.0 - beta_two) * grad * grad
                update = (first * scale_one) / (jnp.sqrt(second * scale_two) + adam_eps)
                updated[at] = (st_w[at] * (1.0 - learn_rate * decay_rate) - update).astype(BF16)
                return inner

            return lax.fori_loop(0, per_dest, one, carry)

        lax.fori_loop(0, groups, group, 0)

    def answer():
        def one(d, carry):
            base = rank_ref[d] * per_dest

            def inner_one(i, inner):
                answers[d * per_dest + i] = updated[base + i]
                return inner

            return lax.fori_loop(0, per_dest, inner_one, carry)

        lax.fori_loop(0, sections, one, 0)

    def placed(c):
        source = returned[c % 2]

        def one(b, carry):
            stage[b] = source[place_ref[b]]
            return carry

        lax.fori_loop(0, 2 * row_blocks, one, 0)
        copy = pltpu.make_async_copy(
            stage, new_out.at[:, :, pl.ds(c * COLS, COLS)], place_sem.at[0]
        )
        copy.start()
        return copy

    def piece_at(ref, i):
        return ref.at[
            pl.ds((i // per_row) * depth, depth), pl.ds((i % per_row) * tok, tok)
        ]

    strip = 256
    strips = depth // strip
    kind_chip = chip_of if folded else [lax.rem(chip + j, chips) for j in range(chips)]

    def strip_of(r):
        return pl.ds(pl.multiple_of(r * strip, strip), strip)

    def cotangent_strip(owner, r):
        t = token_group(owner // split, k)
        half = lax.rem(owner, split)
        start = pl.multiple_of(half * depth + r * strip, strip)
        return jnp.dot(
            w[0, pl.ds(start, strip), :], gathered[t, 0], preferred_element_type=F32
        )

    def kept_strip(j, r):
        owned = cotangent_strip(2 * kind_chip[j] + core, r)
        return owned + from_sibling[j, strip_of(r), :].astype(F32)

    def sibling_piece(j):
        def one(r, carry):
            total = cotangent_strip(2 * kind_chip[j] + 1 - core, r)
            piece_at(act, j)[strip_of(r), :] = total.astype(BF16)
            return carry

        lax.fori_loop(0, strips, one, 0)

    def strip_to(total, j, r, at, peer):
        here = strip_of(r)
        piece_at(cot, j)[here, :] = total.astype(BF16)
        return Pair(
            piece_at(cot, j).at[here, :],
            from_chips.at[at, here, :],
            chip_send.at[at, r],
            chip_recv.at[at, r],
            peer,
        ).start()

    rs = [[] for h in range(HALVES)]
    for i in range(len(order) + 2):
        if i < len(order):
            hops[order[i]].wait_recv()
            if i + AHEAD < len(order):
                go_hop(*order[i + AHEAD])
            first_leg(*order[i])
        if 1 <= i <= len(order):
            second_leg(*order[i - 1])
        if i == 1:
            for copy in loads:
                copy.wait()
            for copy in states_of(0):
                copy.start()
            lifted(0, 0, 1)
        if i >= 2:
            third_leg(*order[i - 2])
            a, d = order[i - 2]
            if a == 1:
                group_done(d)
                lifted(0, ranks - d, ranks - d + 1)
                for h in range(HALVES):
                    rs[h].append(spread_sum(ranks - d, h))
    for copies in (hops, wide, near):
        for copy in copies.values():
            copy.wait_send()
    for copy in counted:
        copy.wait()
    ranking()
    places_of_blocks()
    gathers, outs, rets, places = {}, {}, {}, {}

    def returning(c):
        for copy in outs[c]:
            copy.wait_recv()
        for copy in states_of(c):
            copy.wait()
        adam(c)
        if c + 1 < chunks:
            for copy in states_of(c + 1):
                copy.start()
        if c > 0:
            for copy in rets[c - 1]:
                copy.wait_send()
        answer()
        rets[c] = exchange(answers, returned, ret_send, ret_recv, c)

    def placing(c):
        for copy in rets[c]:
            copy.wait_recv()
        if c > 0:
            places[c - 1].wait()
        places[c] = placed(c)

    for c in range(chunks):
        gathers[c] = []
        for h in range(HALVES):
            for copy in rs[h]:
                copy.wait_recv()
            gated(c, h)
            if c > 0:
                for copy in gathers[c - 1][h]:
                    copy.wait_send()
            gathers[c].append(gather(c, h))
        for half in rs:
            for copy in half:
                copy.wait_send()
        if c + 1 < chunks:
            lifted(c + 1, 0, ranks)
        if c > 1:
            placing(c - 2)
        if c > 0:
            returning(c - 1)
        rs = []
        for half in gathers[c]:
            for copy in half:
                copy.wait_recv()
            if c + 1 < chunks:
                rs.append([spread_sum(d, len(rs)) for d in range(1, ranks)])
        if c > 0:
            for copy in outs[c - 1]:
                copy.wait_send()
        gradients(c)
        if c + 1 < chunks:
            outs[c] = exchange(outgoing, arrivals, out_send, out_recv, c)

    to_sibling = []
    for j in list(range(1, chips)) + [0]:
        sibling_piece(j)
        to_sibling.append(
            Pair(
                piece_at(act, j), from_sibling.at[j], sib_send.at[j], sib_recv.at[j], sibling
            ).start()
        )
    for copy in to_sibling:
        copy.wait_recv()
    to_chips = {}
    for r in range(strips):
        if folded:
            near_kind = 1 + r % 2
            for at, j in enumerate((near_kind, 3)):
                to_chips[at, r] = strip_to(kept_strip(j, r), j, r, at, reach[near_kind])
        else:
            for j in range(1, chips):
                to_chips[j - 1, r] = strip_to(kept_strip(j, r), j, r, j - 1, across[j])
    if chunks > 1:
        placing(chunks - 2)
    if folded:
        for r in range(strips):
            far_kind = 2 - r % 2
            to_chips[1, r].wait_recv()
            total = kept_strip(far_kind, r) + from_chips[1, strip_of(r), :].astype(F32)
            to_chips[2, r] = strip_to(total, far_kind, r, 2, reach[far_kind])
    outs[chunks - 1] = exchange(outgoing, arrivals, out_send, out_recv, chunks - 1)
    returning(chunks - 1)
    for copy in to_sibling:
        copy.wait_send()
    result = act.at[pl.ds((ranks - 1) * tok, tok), pl.ds(0, depth)]
    lasts = []
    for r in range(strips):
        total = kept_strip(0, r)
        for j in range(chips - 1):
            if not (folded and j == 1):
                to_chips[j, r].wait_recv()
                total += from_chips[j, strip_of(r), :].astype(F32)
        result[:, r * strip : (r + 1) * strip] = total.T.astype(BF16)
        there = pl.ds(r * strip, strip)
        last = Pair(
            result.at[:, there],
            back_out.at[:, there],
            last_send.at[r],
            last_recv.at[r],
            (target_section, group_here),
        )
        kept = pltpu.make_async_copy(
            result.at[:, there], back_out.at[:, there], kept_sem.at[r]
        )
        lasts.append((last, kept))

        @pl.when(jnp.logical_not(stays))
        def _():
            last.start()

        @pl.when(stays)
        def _():
            kept.start()

    placing(chunks - 1)

    @pl.when(jnp.logical_not(stays))
    def _():
        for last, kept in lasts:
            last.copy.wait()

    @pl.when(stays)
    def _():
        for last, kept in lasts:
            kept.wait()

    for copy in to_chips.values():
        copy.wait_send()
    for copies in (*gathers[chunks - 1], outs[chunks - 1], rets[chunks - 1]):
        for copy in copies:
            copy.wait_send()
    places[chunks - 1].wait()


def layer(owners, adam_step, activations, cotangent, weights, gate_pre, states, sections, ranks, per_dest):
    row_count = weights.shape[1]
    tok, units = gate_pre.shape
    tokens = tok * ranks
    capacity, rows = states[0].shape[:2]
    groups = capacity // per_dest
    chips = sections // 2
    depth = row_count * ranks // sections
    strips = depth // 256
    blocks = 2 * row_count // rows
    slots = sections * per_dest
    anywhere = pl.BlockSpec(memory_space=pl.ANY)
    scalars = pl.BlockSpec(memory_space=pltpu.SMEM)
    shape = (sections, ranks, tok, units, row_count, rows, per_dest, groups)

    def body(*refs):
        layer_kernel(shape, *refs)

    sems = pltpu.SemaphoreType.DMA
    flops = 2 * tokens * row_count * units * 5
    return pl.pallas_call(
        body,
        out_shape=(
            jax.ShapeDtypeStruct((tok, depth), BF16),
            jax.ShapeDtypeStruct((blocks, rows, units), BF16),
        ),
        in_specs=[scalars] * 2 + [anywhere] * 7,
        out_specs=(anywhere, anywhere),
        scratch_shapes=[
            pltpu.VMEM((tokens, row_count), BF16),
            pltpu.VMEM((tokens, row_count), BF16),
            pltpu.VMEM(weights.shape, BF16),
            pltpu.VMEM((tok, units), BF16),
            pltpu.VMEM((ranks, tok, 2 * COLS), BF16),
            pltpu.VMEM((ranks - 1, tok, 2 * COLS), BF16),
            pltpu.VMEM((ranks, 2, units, tok), BF16),
            pltpu.VMEM((blocks, rows, COLS), BF16),
            pltpu.VMEM((slots, rows, COLS), BF16),
            pltpu.VMEM((slots, rows, COLS), BF16),
            pltpu.VMEM((slots, rows, COLS), BF16),
            pltpu.VMEM((capacity, rows, COLS), BF16),
            pltpu.VMEM((slots, rows, COLS), BF16),
            pltpu.VMEM((slots, rows, COLS), BF16),
            pltpu.VMEM((slots, rows, COLS), BF16),
            pltpu.VMEM((capacity, rows, COLS), F32),
            pltpu.VMEM((capacity, rows, COLS), F32),
            pltpu.VMEM((capacity, rows, COLS), F32),
            pltpu.VMEM((blocks, rows, COLS), BF16),
            pltpu.VMEM((chips, depth, tok), BF16),
            pltpu.VMEM((chips - 1, depth, tok), BF16),
            pltpu.VMEM((8, 128), jnp.int32),
            pltpu.VMEM((sections, 8, 128), jnp.int32),
            pltpu.SMEM((slots,), jnp.int32),
            pltpu.SMEM((blocks,), jnp.int32),
            pltpu.SMEM((groups,), jnp.int32),
            pltpu.SMEM((sections,), jnp.int32),
            sems((5,)),
            sems((3,)),
            sems((2,)),
            sems((1,)),
            sems((sections - 1,)),
            sems((sections - 1,)),
            sems((2, ranks - 1)),
            sems((2, ranks - 1)),
            sems((2, ranks - 1, chips - 1)),
            sems((2, ranks - 1, chips - 1)),
            sems((2, ranks - 1, chips)),
            sems((2, ranks - 1, chips)),
            sems((HALVES, ranks - 1)),
            sems((HALVES, ranks - 1)),
            sems((HALVES, ranks - 1)),
            sems((HALVES, ranks - 1)),
            sems((sections - 1,)),
            sems((2, sections - 1)),
            sems((sections - 1,)),
            sems((2, sections - 1)),
            sems((chips,)),
            sems((chips,)),
            sems((chips - 1, strips)),
            sems((chips - 1, strips)),
            sems((strips,)),
            sems((strips,)),
            sems((strips,)),
        ],
        compiler_params=pltpu.CompilerParams(
            collective_id=2, has_side_effects=True, vmem_limit_bytes=VMEM_BYTES
        ),
        cost_estimate=pl.CostEstimate(
            flops=flops, bytes_accessed=12 * capacity * rows * units, transcendentals=0
        ),
        name="layer",
    )(owners, adam_step, activations, cotangent, weights, gate_pre, *states)


def per_device(
    activations, cotangent, gate_pre, weights, holder_map, master, moment_one, moment_two, adam_step
):
    sections = lax.axis_size("section")
    ranks = lax.axis_size("dp")
    row_count, hidden_units = weights.shape[1:]
    block_rows = master.shape[3]
    row_blocks = row_count // block_rows
    per_dest = 4 * row_blocks // sections

    owners = holder_map[:, 0, :].reshape(-1)
    states = (master[0, 0], moment_one[0, 0], moment_two[0, 0])
    passed_back, blocks = layer(
        owners,
        adam_step,
        activations,
        cotangent,
        weights,
        gate_pre,
        states,
        sections,
        ranks,
        per_dest,
    )
    return (passed_back, blocks.reshape(weights.shape))


def solution(mesh):
    in_specs = (
        P("dp", None),
        P("dp", None),
        P("dp", "section"),
        P(None, "dp", "section"),
        P("dp", "section", None),
        P("section", "dp", None, None, None),
        P("section", "dp", None, None, None),
        P("section", "dp", None, None, None),
        P(),
    )
    out_specs = (P("dp", "section"), P(None, "dp", "section"))
    return jax.shard_map(
        per_device, mesh=mesh, in_specs=in_specs, out_specs=out_specs, check_vma=False
    )
```

```python
import math

import jax
import jax.numpy as jnp
from jax import lax
from jax.experimental import pallas as pl
from jax.experimental.pallas import tpu as pltpu
from jax.sharding import PartitionSpec as P

learn_rate = 0.03
beta_one = 0.9
beta_two = 0.95
adam_eps = 1e-08
decay_rate = 0.1

BF16 = jnp.bfloat16
F32 = jnp.float32


COLS = 128
AHEAD = 2
HALVES = 2
VMEM_BYTES = 62 * 2**20
MESH = pl.DeviceIdType.MESH


class Pair:
    def __init__(self, src, dst, send_sem, recv_sem, peer):
        self.copy = pltpu.make_async_remote_copy(
            src_ref=src,
            dst_ref=dst,
            send_sem=send_sem,
            recv_sem=recv_sem,
            device_id=peer,
            device_id_type=MESH,
        )

    def start(self):
        self.copy.start()
        return self.copy


def layer_kernel(
    shape,
    owner_ref,
    step_ref,
    act_hbm,
    cot_hbm,
    w_hbm,
    gate_hbm,
    master_hbm,
    first_hbm,
    second_hbm,
    back_out,
    new_out,
    act,
    cot,
    w,
    gate,
    part,
    landed,
    gathered,
    grads,
    outgoing,
    arrivals_even,
    arrivals_odd,
    updated,
    answers,
    returned_even,
    returned_odd,
    st_w,
    st_a,
    st_b,
    stage,
    from_sibling,
    from_chips,
    counts,
    table,
    pick_ref,
    place_ref,
    source_ref,
    rank_ref,
    load_sem,
    state_sem,
    local_sem,
    place_sem,
    count_send,
    count_recv,
    hop_send,
    hop_recv,
    wide_send,
    wide_recv,
    near_send,
    near_recv,
    rs_send,
    rs_recv,
    ag_send,
    ag_recv,
    out_send,
    out_recv,
    ret_send,
    ret_recv,
    sib_send,
    sib_recv,
    chip_send,
    chip_recv,
    last_send,
    last_recv,
    kept_sem,
):
    sections, ranks, tok, units, row_count, rows, per_dest, groups = shape
    arrivals = (arrivals_even, arrivals_odd)
    returned = (returned_even, returned_odd)
    chunks = units // COLS
    chips = sections // 2
    split = sections // ranks
    depth = row_count // split
    row_blocks = row_count // rows
    per_row = row_count // tok
    s = lax.axis_index("section")
    k = lax.axis_index("dp")
    core = lax.rem(s, 2)
    chip = s // 2
    sibling = (s + 1 - 2 * core, k)
    along = [(s, lax.rem(k + d, ranks)) for d in range(ranks)]
    plane = [(lax.rem(s + e, sections), k) for e in range(sections)]
    across = [(2 * lax.rem(chip + j, chips) + core, k) for j in range(chips)]
    if ranks == 4:

        def token_group(part, rank):
            low = lax.rem(rank // 2 + lax.rem(part, 2), 2)
            return 2 * lax.rem(lax.rem(rank, 2) + part // 2, 2) + low

        part_of = token_group
    else:

        def token_group(part, rank):
            return lax.rem(part + rank, ranks)

        def part_of(group, rank):
            return lax.rem(group + ranks - rank, ranks)

    group_here = token_group(s // split, k)
    target_section = split * k + lax.rem(s, split)
    group_back = part_of(k, s // split)
    origin = (split * group_back + lax.rem(s, split), s // split)
    stays = (target_section == s) & (group_here == k)

    loads = []

    def load(src, dst):
        copy = pltpu.make_async_copy(src, dst, load_sem.at[len(loads)])
        copy.start()
        loads.append(copy)

    own_cols = pl.ds(pl.multiple_of(k * row_count, row_count), row_count)
    own_rows = pl.ds(pl.multiple_of(k * tok, tok), tok)
    load(w_hbm, w)
    load(cot_hbm.at[:, own_cols], cot.at[own_rows, :])
    load(act_hbm.at[:, own_cols], act.at[own_rows, :])
    load(gate_hbm, gate)
    lanes = lax.broadcasted_iota(jnp.int32, counts.shape, 1)
    held = jnp.zeros(counts.shape, jnp.int32)
    for b in range(2 * row_blocks):
        held += (lanes == owner_ref[b]).astype(jnp.int32)
    counts[...] = held
    load(counts, table.at[s])

    def states_of(c):
        at = pl.ds(c * COLS, COLS)
        return [
            pltpu.make_async_copy(src.at[:, :, at], dst, state_sem.at[i])
            for i, (src, dst) in enumerate(
                ((master_hbm, st_w), (first_hbm, st_a), (second_hbm, st_b))
            )
        ]

    barrier = pltpu.get_barrier_semaphore()
    greeted = along[1:] + plane[1:]
    for peer in greeted:
        pl.semaphore_signal(barrier, inc=1, device_id=peer, device_id_type=MESH)

    @pl.when(jnp.logical_not(stays))
    def _():
        for peer in ((target_section, group_here), origin):
            pl.semaphore_signal(barrier, inc=1, device_id=peer, device_id_type=MESH)

    pl.semaphore_wait(barrier, jnp.where(stays, len(greeted), len(greeted) + 2))
    piece = tok // sections
    pairs = ((cot_hbm, cot), (act_hbm, act))
    folded = chips == 4
    if folded:
        chip_of = (chip, chip + 1 - 2 * lax.rem(chip, 2), lax.rem(chip + 2, 4), 3 - chip)
        reach = {kind: (2 * chip_of[kind] + core, k) for kind in (1, 2)}
    else:
        chip_of = [lax.rem(chip + chips - j, chips) for j in range(chips)]
        reach = {kind: across[kind] for kind in range(1, chips)}

    def block_of(a, d, kind):
        rank = lax.rem(k + ranks - d, ranks)
        start = pl.multiple_of(rank * tok + (2 * chip_of[kind] + core) * piece, piece)
        return pairs[a][1].at[pl.ds(start, piece), :]

    hops, wide, near = {}, {}, {}
    order = [
        (a, d)
        for d in sorted(range(1, ranks), key=lambda d: (min(d, ranks - d), d))
        for a in range(2)
    ]

    def go_hop(a, d):
        from_rows = pl.ds(pl.multiple_of(s * piece, piece), piece)
        cols = pl.ds(pl.multiple_of(along[d][1] * row_count, row_count), row_count)
        hops[a, d] = Pair(
            pairs[a][0].at[from_rows, cols],
            block_of(a, 0, 0),
            hop_send.at[a, d - 1],
            hop_recv.at[a, d - 1],
            along[d],
        ).start()

    for a, d in order[:AHEAD]:
        go_hop(a, d)
    counted = [
        Pair(
            counts, table.at[s], count_send.at[e - 1], count_recv.at[e - 1], plane[e]
        ).start()
        for e in range(1, sections)
    ]

    def go_wide(a, d, kind, block, peer):
        at = (a, d - 1, kind - 1)
        wide[a, d, kind] = Pair(block, block, wide_send.at[at], wide_recv.at[at], peer).start()

    def go_near(a, d, kind, block):
        at = (a, d - 1, kind)
        near[a, d, kind] = Pair(block, block, near_send.at[at], near_recv.at[at], sibling).start()

    def first_leg(a, d):
        block = block_of(a, d, 0)
        for kind, peer in reach.items():
            go_wide(a, d, kind, block, peer)
        go_near(a, d, 0, block)

    def second_leg(a, d):
        for kind in reach:
            wide[a, d, kind].wait_recv()
            block = block_of(a, d, kind)
            if folded and kind == 1 + a:
                go_wide(a, d, 3, block, reach[2 - a])
            go_near(a, d, kind, block)

    def third_leg(a, d):
        if folded:
            wide[a, d, 3].wait_recv()
            go_near(a, d, 3, block_of(a, d, 3))

    def group_done(d):
        for a in range(2):
            for kind in range(chips):
                near[a, d, kind].wait_recv()

    def lifted(c, first, last):
        at = slice(c * COLS, (c + 1) * COLS)

        def one(d, carry):
            t_rows = pl.ds(pl.multiple_of(lax.rem(k + d, ranks) * tok, tok), tok)
            part[d, :, :COLS] = jnp.dot(
                cot[t_rows, :], w[1, :, at], preferred_element_type=F32
            ).astype(BF16)
            part[d, :, COLS:] = jnp.dot(
                act[t_rows, :], w[0, :, at], preferred_element_type=F32
            ).astype(BF16)
            return carry

        lax.fori_loop(first, last, one, 0)

    half_tok = tok // HALVES

    def half_of(h):
        return slice(h * half_tok, (h + 1) * half_tok)

    def spread_sum(d, h):
        here = pl.ds(h * half_tok, half_tok)
        return Pair(
            part.at[d, here, :],
            landed.at[d - 1, here, :],
            rs_send.at[h, d - 1],
            rs_recv.at[h, d - 1],
            along[d],
        ).start()

    def gated(c, h):
        at = slice(c * COLS, (c + 1) * COLS)
        here = half_of(h)
        g = gate[here, at].astype(F32)
        silu = g / (1.0 + jnp.exp(-g))
        for m in range(2):
            cols = slice(m * COLS, (m + 1) * COLS)
            total = part[0, here, cols].astype(F32)
            for d in range(1, ranks):
                total += landed[d - 1, here, cols].astype(F32)
            gathered[k, m, at, here] = (total * silu).T.astype(BF16)

    def gather(c, h):
        block = gathered.at[k, :, pl.ds(c * COLS, COLS), pl.ds(h * half_tok, half_tok)]
        return [
            Pair(block, block, ag_send.at[h, d - 1], ag_recv.at[h, d - 1], along[d]).start()
            for d in range(1, ranks)
        ]

    def gradients(c):
        at = slice(c * COLS, (c + 1) * COLS)
        tile = 2 * rows

        def one(j, carry):
            cols = pl.ds(pl.multiple_of(j * tile, tile), tile)
            for m, ref in enumerate((act, cot)):
                total = jnp.zeros((COLS, tile), F32)
                for t in range(ranks):
                    total += jnp.dot(
                        gathered[t, m, at, :],
                        ref[t * tok : (t + 1) * tok, cols],
                        preferred_element_type=F32,
                    )
                for b in range(2):
                    block = total[:, b * rows : (b + 1) * rows]
                    grads[m * row_blocks + 2 * j + b] = block.T.astype(BF16)
            return carry

        lax.fori_loop(0, row_blocks // 2, one, 0)

        def pick(q, carry):
            outgoing[q] = grads[pick_ref[q]]
            return carry

        lax.fori_loop(0, sections * per_dest, pick, 0)

    def slots(ref, section):
        return ref.at[pl.ds(section * per_dest, per_dest)]

    def exchange(src, dst, sends, recvs, c):
        copies = [
            Pair(
                slots(src, plane[e][0]),
                slots(dst[c % 2], s),
                sends.at[e - 1],
                recvs.at[c % 2, e - 1],
                plane[e],
            ).start()
            for e in range(sections - 1, 0, -1)
        ]
        own = pltpu.make_async_copy(slots(src, s), slots(dst[c % 2], s), local_sem.at[0])
        own.start()
        own.wait()
        return copies

    def places_of_blocks():
        count = 2 * row_blocks

        def one(b, carry):
            owner = owner_ref[b]
            order_in = jnp.int32(0)
            for other in range(count):
                order_in += jnp.where((owner_ref[other] == owner) & (other < b), 1, 0)
            place_ref[lax.rem(b, 2) * row_blocks + b // 2] = owner * per_dest + order_in
            return carry

        lax.fori_loop(0, count, one, 0)

        def back(q, carry):
            block = jnp.int32(0)
            for b in range(count):
                block += jnp.where(place_ref[b] == q, b, 0)
            pick_ref[q] = block
            return carry

        lax.fori_loop(0, sections * per_dest, back, 0)

    def ranking():
        lane = lax.broadcasted_iota(jnp.int32, (1, 128), 1)
        lives = [
            (jnp.sum(jnp.where(lane == s, table[p, 0:1, :], 0)) > 0).astype(jnp.int32)
            for p in range(sections)
        ]
        before = jnp.int32(0)
        sources = [jnp.int32(0)] * groups
        for p in range(sections):
            rank_ref[p] = jnp.minimum(before, groups - 1)
            for g in range(groups):
                sources[g] += jnp.where(before == g, lives[p] * p, 0)
            before += lives[p]
        for g in range(groups):
            source_ref[g] = sources[g]

    def adam(c):
        step = jnp.full((1, COLS), step_ref[0].astype(F32), F32)
        scale_one = learn_rate / (1.0 - jnp.exp(step * math.log(beta_one)))
        scale_two = 1.0 / (1.0 - jnp.exp(step * math.log(beta_two)))
        arrived = arrivals[c % 2]

        def group(g, carry):
            base = source_ref[g] * per_dest

            def one(i, inner):
                at = g * per_dest + i
                grad = arrived[base + i].astype(F32)
                first = beta_one * st_a[at] + (1.0 - beta_one) * grad
                second = beta_two * st_b[at] + (1.0 - beta_two) * grad * grad
                update = (first * scale_one) / (jnp.sqrt(second * scale_two) + adam_eps)
                updated[at] = (st_w[at] * (1.0 - learn_rate * decay_rate) - update).astype(BF16)
                return inner

            return lax.fori_loop(0, per_dest, one, carry)

        lax.fori_loop(0, groups, group, 0)

    def answer():
        def one(d, carry):
            base = rank_ref[d] * per_dest

            def inner_one(i, inner):
                answers[d * per_dest + i] = updated[base + i]
                return inner

            return lax.fori_loop(0, per_dest, inner_one, carry)

        lax.fori_loop(0, sections, one, 0)

    def placed(c):
        source = returned[c % 2]

        def one(b, carry):
            stage[b] = source[place_ref[b]]
            return carry

        lax.fori_loop(0, 2 * row_blocks, one, 0)
        copy = pltpu.make_async_copy(
            stage, new_out.at[:, :, pl.ds(c * COLS, COLS)], place_sem.at[0]
        )
        copy.start()
        return copy

    def piece_at(ref, i):
        return ref.at[
            pl.ds((i // per_row) * depth, depth), pl.ds((i % per_row) * tok, tok)
        ]

    strip = 256
    strips = depth // strip
    kind_chip = chip_of if folded else [lax.rem(chip + j, chips) for j in range(chips)]

    def strip_of(r):
        return pl.ds(pl.multiple_of(r * strip, strip), strip)

    def cotangent_strip(owner, r):
        t = token_group(owner // split, k)
        half = lax.rem(owner, split)
        start = pl.multiple_of(half * depth + r * strip, strip)
        return jnp.dot(
            w[0, pl.ds(start, strip), :], gathered[t, 0], preferred_element_type=F32
        )

    def kept_strip(j, r):
        owned = cotangent_strip(2 * kind_chip[j] + core, r)
        return owned + from_sibling[j, strip_of(r), :].astype(F32)

    def sibling_piece(j):
        def one(r, carry):
            total = cotangent_strip(2 * kind_chip[j] + 1 - core, r)
            piece_at(act, j)[strip_of(r), :] = total.astype(BF16)
            return carry

        lax.fori_loop(0, strips, one, 0)

    def strip_to(total, j, r, at, peer):
        here = strip_of(r)
        piece_at(cot, j)[here, :] = total.astype(BF16)
        return Pair(
            piece_at(cot, j).at[here, :],
            from_chips.at[at, here, :],
            chip_send.at[at, r],
            chip_recv.at[at, r],
            peer,
        ).start()

    rs = [[] for h in range(HALVES)]
    for i in range(len(order) + 2):
        if i < len(order):
            hops[order[i]].wait_recv()
            if i + AHEAD < len(order):
                go_hop(*order[i + AHEAD])
            first_leg(*order[i])
        if 1 <= i <= len(order):
            second_leg(*order[i - 1])
        if i == 1:
            for copy in loads:
                copy.wait()
            for copy in states_of(0):
                copy.start()
            lifted(0, 0, 1)
        if i >= 2:
            third_leg(*order[i - 2])
            a, d = order[i - 2]
            if a == 1:
                group_done(d)
                lifted(0, ranks - d, ranks - d + 1)
                for h in range(HALVES):
                    rs[h].append(spread_sum(ranks - d, h))
    for copies in (hops, wide, near):
        for copy in copies.values():
            copy.wait_send()
    for copy in counted:
        copy.wait()
    ranking()
    places_of_blocks()
    gathers, outs, rets, places = {}, {}, {}, {}

    def returning(c):
        for copy in outs[c]:
            copy.wait_recv()
        for copy in states_of(c):
            copy.wait()
        adam(c)
        if c + 1 < chunks:
            for copy in states_of(c + 1):
                copy.start()
        if c > 0:
            for copy in rets[c - 1]:
                copy.wait_send()
        answer()
        rets[c] = exchange(answers, returned, ret_send, ret_recv, c)

    def placing(c):
        for copy in rets[c]:
            copy.wait_recv()
        if c > 0:
            places[c - 1].wait()
        places[c] = placed(c)

    for c in range(chunks):
        gathers[c] = []
        for h in range(HALVES):
            for copy in rs[h]:
                copy.wait_recv()
            gated(c, h)
            if c > 0:
                for copy in gathers[c - 1][h]:
                    copy.wait_send()
            gathers[c].append(gather(c, h))
        for half in rs:
            for copy in half:
                copy.wait_send()
        if c + 1 < chunks:
            lifted(c + 1, 0, ranks)
        if c > 1:
            placing(c - 2)
        if c > 0:
            returning(c - 1)
        rs = []
        for half in gathers[c]:
            for copy in half:
                copy.wait_recv()
            if c + 1 < chunks:
                rs.append([spread_sum(d, len(rs)) for d in range(1, ranks)])
        if c > 0:
            for copy in outs[c - 1]:
                copy.wait_send()
        gradients(c)
        if c + 1 < chunks:
            outs[c] = exchange(outgoing, arrivals, out_send, out_recv, c)

    to_sibling = []
    for j in list(range(1, chips)) + [0]:
        sibling_piece(j)
        to_sibling.append(
            Pair(
                piece_at(act, j), from_sibling.at[j], sib_send.at[j], sib_recv.at[j], sibling
            ).start()
        )
    for copy in to_sibling:
        copy.wait_recv()
    to_chips = {}
    for r in range(strips):
        if folded:
            near_kind = 1 + r % 2
            for at, j in enumerate((near_kind, 3)):
                to_chips[at, r] = strip_to(kept_strip(j, r), j, r, at, reach[near_kind])
        else:
            for j in range(1, chips):
                to_chips[j - 1, r] = strip_to(kept_strip(j, r), j, r, j - 1, across[j])
    if chunks > 1:
        placing(chunks - 2)
    if folded:
        for r in range(strips):
            far_kind = 2 - r % 2
            to_chips[1, r].wait_recv()
            total = kept_strip(far_kind, r) + from_chips[1, strip_of(r), :].astype(F32)
            to_chips[2, r] = strip_to(total, far_kind, r, 2, reach[far_kind])
    outs[chunks - 1] = exchange(outgoing, arrivals, out_send, out_recv, chunks - 1)
    returning(chunks - 1)
    for copy in to_sibling:
        copy.wait_send()
    result = act.at[pl.ds((ranks - 1) * tok, tok), pl.ds(0, depth)]
    lasts = []
    for r in range(strips):
        total = kept_strip(0, r)
        for j in range(chips - 1):
            if not (folded and j == 1):
                to_chips[j, r].wait_recv()
                total += from_chips[j, strip_of(r), :].astype(F32)
        result[:, r * strip : (r + 1) * strip] = total.T.astype(BF16)
        there = pl.ds(r * strip, strip)
        last = Pair(
            result.at[:, there],
            back_out.at[:, there],
            last_send.at[r],
            last_recv.at[r],
            (target_section, group_here),
        )
        kept = pltpu.make_async_copy(
            result.at[:, there], back_out.at[:, there], kept_sem.at[r]
        )
        lasts.append((last, kept))

        @pl.when(jnp.logical_not(stays))
        def _():
            last.start()

        @pl.when(stays)
        def _():
            kept.start()

    placing(chunks - 1)

    @pl.when(jnp.logical_not(stays))
    def _():
        for last, kept in lasts:
            last.copy.wait()

    @pl.when(stays)
    def _():
        for last, kept in lasts:
            kept.wait()

    for copy in to_chips.values():
        copy.wait_send()
    for copies in (*gathers[chunks - 1], outs[chunks - 1], rets[chunks - 1]):
        for copy in copies:
            copy.wait_send()
    places[chunks - 1].wait()


def layer(owners, adam_step, activations, cotangent, weights, gate_pre, states, sections, ranks, per_dest):
    row_count = weights.shape[1]
    tok, units = gate_pre.shape
    tokens = tok * ranks
    capacity, rows = states[0].shape[:2]
    groups = capacity // per_dest
    chips = sections // 2
    depth = row_count * ranks // sections
    strips = depth // 256
    blocks = 2 * row_count // rows
    slots = sections * per_dest
    anywhere = pl.BlockSpec(memory_space=pl.ANY)
    scalars = pl.BlockSpec(memory_space=pltpu.SMEM)
    shape = (sections, ranks, tok, units, row_count, rows, per_dest, groups)

    def body(*refs):
        layer_kernel(shape, *refs)

    sems = pltpu.SemaphoreType.DMA
    flops = 2 * tokens * row_count * units * 5
    return pl.pallas_call(
        body,
        out_shape=(
            jax.ShapeDtypeStruct((tok, depth), BF16),
            jax.ShapeDtypeStruct((blocks, rows, units), BF16),
        ),
        in_specs=[scalars] * 2 + [anywhere] * 7,
        out_specs=(anywhere, anywhere),
        scratch_shapes=[
            pltpu.VMEM((tokens, row_count), BF16),
            pltpu.VMEM((tokens, row_count), BF16),
            pltpu.VMEM(weights.shape, BF16),
            pltpu.VMEM((tok, units), BF16),
            pltpu.VMEM((ranks, tok, 2 * COLS), BF16),
            pltpu.VMEM((ranks - 1, tok, 2 * COLS), BF16),
            pltpu.VMEM((ranks, 2, units, tok), BF16),
            pltpu.VMEM((blocks, rows, COLS), BF16),
            pltpu.VMEM((slots, rows, COLS), BF16),
            pltpu.VMEM((slots, rows, COLS), BF16),
            pltpu.VMEM((slots, rows, COLS), BF16),
            pltpu.VMEM((capacity, rows, COLS), BF16),
            pltpu.VMEM((slots, rows, COLS), BF16),
            pltpu.VMEM((slots, rows, COLS), BF16),
            pltpu.VMEM((slots, rows, COLS), BF16),
            pltpu.VMEM((capacity, rows, COLS), F32),
            pltpu.VMEM((capacity, rows, COLS), F32),
            pltpu.VMEM((capacity, rows, COLS), F32),
            pltpu.VMEM((blocks, rows, COLS), BF16),
            pltpu.VMEM((chips, depth, tok), BF16),
            pltpu.VMEM((chips - 1, depth, tok), BF16),
            pltpu.VMEM((8, 128), jnp.int32),
            pltpu.VMEM((sections, 8, 128), jnp.int32),
            pltpu.SMEM((slots,), jnp.int32),
            pltpu.SMEM((blocks,), jnp.int32),
            pltpu.SMEM((groups,), jnp.int32),
            pltpu.SMEM((sections,), jnp.int32),
            sems((5,)),
            sems((3,)),
            sems((2,)),
            sems((1,)),
            sems((sections - 1,)),
            sems((sections - 1,)),
            sems((2, ranks - 1)),
            sems((2, ranks - 1)),
            sems((2, ranks - 1, chips - 1)),
            sems((2, ranks - 1, chips - 1)),
            sems((2, ranks - 1, chips)),
            sems((2, ranks - 1, chips)),
            sems((HALVES, ranks - 1)),
            sems((HALVES, ranks - 1)),
            sems((HALVES, ranks - 1)),
            sems((HALVES, ranks - 1)),
            sems((sections - 1,)),
            sems((2, sections - 1)),
            sems((sections - 1,)),
            sems((2, sections - 1)),
            sems((chips,)),
            sems((chips,)),
            sems((chips - 1, strips)),
            sems((chips - 1, strips)),
            sems((strips,)),
            sems((strips,)),
            sems((strips,)),
        ],
        compiler_params=pltpu.CompilerParams(
            collective_id=2, has_side_effects=True, vmem_limit_bytes=VMEM_BYTES
        ),
        cost_estimate=pl.CostEstimate(
            flops=flops, bytes_accessed=12 * capacity * rows * units, transcendentals=0
        ),
        name="layer",
    )(owners, adam_step, activations, cotangent, weights, gate_pre, *states)


def per_device(
    activations, cotangent, gate_pre, weights, holder_map, master, moment_one, moment_two, adam_step
):
    sections = lax.axis_size("section")
    ranks = lax.axis_size("dp")
    row_count, hidden_units = weights.shape[1:]
    block_rows = master.shape[3]
    row_blocks = row_count // block_rows
    per_dest = 4 * row_blocks // sections

    owners = holder_map[:, 0, :].reshape(-1)
    states = (master[0, 0], moment_one[0, 0], moment_two[0, 0])
    passed_back, blocks = layer(
        owners,
        adam_step,
        activations,
        cotangent,
        weights,
        gate_pre,
        states,
        sections,
        ranks,
        per_dest,
    )
    return (passed_back, blocks.reshape(weights.shape))


def solution(mesh):
    in_specs = (
        P("dp", None),
        P("dp", None),
        P("dp", "section"),
        P(None, "dp", "section"),
        P("dp", "section", None),
        P("section", "dp", None, None, None),
        P("section", "dp", None, None, None),
        P("section", "dp", None, None, None),
        P(),
    )
    out_specs = (P("dp", "section"), P(None, "dp", "section"))
    return jax.shard_map(
        per_device, mesh=mesh, in_specs=in_specs, out_specs=out_specs, check_vma=False
    )
```
